32 devices in a mesh: patch: 2 (over x), epoch: 8 (over z, y), tile: 2 (over core).
Axes of the slice: x: 2, y: 2, z: 4, core: 2. Of those that a mesh axis runs over, the one named last changes fastest.
Arguments:
- template: float32 [1024, 1024], P(('patch', 'tile'), 'epoch'), parts along dimension 0, may hold values from -6 to 6
- science: float32 [16, 512, 1024], P(('patch', 'epoch'), 'tile'), parts along dimension 0, may hold values from -6 to 6, as said below
- flags: int32 [16, 512, 1024], P(('patch', 'epoch'), 'tile'), parts along dimension 0, may hold values 0 or 1
- stamp_rows: int32 [16, 32], P(('patch', 'epoch'), 'tile'), parts along dimension 0, may hold values from 0 to 224
- stamp_cols: int32 [16, 32], P(('patch', 'epoch'), 'tile'), parts along dimension 0, may hold values from 0 to 992
Outputs:
- detection: float32 [16, 512, 1024], P(('patch', 'epoch'), 'tile'), parts along dimension 0
- coefficients: float32 [24], P('patch'), parts along dimension 0
The draws below stay inside these ranges and needn't reach their ends.
There are 2 independent parts, one for each index of `patch`. The reference program is written for one: setup_inputs(seed, part) draws one part's arguments, and reference() takes and returns one part's arrays. A program takes and returns all parts, laid end to end along the dimension named above; each array names one. Nothing has to cross between parts.
Inputs may be any that keep to these rules, and one draw needn't show every extreme that they name: `stamp_rows`: stamps lie inside their tile. `stamp_cols`: stamps lie inside the image. `science`: each exposure is the template matched by some kernel, plus noise.
All inputs are finite; a program needn't handle non-finite values. No bound on the sum of `flags` on one device may be relied on, other than what follows from the above.
Results may differ from the reference program's by a relative error of at most 0.0003.
Values sent between devices are 32-bit elements; how exact they have to be, the bound alone decides.
A program may use at most 128 MiB of HBM per device.

```python
import jax
import jax.numpy as jnp
from jax import lax

R_DEV = 256
COLS = 1024
STAMPS_DEV = 16
STAMP = 32
NBASIS = 12
ROWS = 512
EPOCHS = 8
STAMPS = 32


def draw_profiles():
    offsets = jnp.arange(15, dtype=jnp.float32) - 7.0
    row_list = []
    col_list = []
    for sigma in (1.0, 2.0, 3.5):
        gauss = jnp.exp(-offsets * offsets / (2.0 * sigma * sigma))
        gauss = gauss / jnp.sum(gauss)
        for power_r, power_c in ((0, 0), (1, 0), (0, 1), (1, 1)):
            row_list.append(gauss * (offsets / 7.0) if power_r else gauss)
            col_list.append(gauss * (offsets / 7.0) if power_c else gauss)
    return (jnp.stack(row_list), jnp.stack(col_list))


def draw_rows_conv(extended, profile):
    count = extended.shape[0] - 14
    total = jnp.zeros((profile.shape[0], count, extended.shape[1]), jnp.float32)
    for shift in range(15):
        total = total + profile[:, shift, None, None] * extended[None, shift:shift + count, :]
    return total


def draw_cols_conv(extended, profile):
    count = extended.shape[2] - 14
    total = jnp.zeros((profile.shape[0], extended.shape[1], count), jnp.float32)
    for shift in range(15):
        total = total + profile[:, shift, None, None] * extended[:, :, shift:shift + count]
    return total


def template_field(key):
    field = jax.random.normal(jax.random.fold_in(key, 101), (ROWS, COLS), jnp.float32)
    return jnp.clip(field, -6.0, 6.0)


def draw_template(key, part):
    return template_field(key)


def draw_science(key, part):
    field = template_field(key)
    row_prof, col_prof = draw_profiles()
    images = draw_cols_conv(draw_rows_conv(jnp.pad(field, 7), row_prof), col_prof)
    mixing = 0.15 * jax.random.normal(jax.random.fold_in(key, 201), (EPOCHS, 12), jnp.float32)
    mixing = mixing + jax.nn.one_hot(4, 12, dtype=jnp.float32)[None, :]
    blurred = jnp.einsum('ek,krc->erc', mixing, images, precision=lax.Precision.HIGHEST)
    noise = 0.08 * jax.random.normal(jax.random.fold_in(key, 202), (EPOCHS, ROWS, COLS), jnp.float32)
    return jnp.clip(blurred + noise, -6.0, 6.0)


def plant(array, rng, low, high):
    place = [jax.random.randint(jax.random.fold_in(rng, axis), (), 0, length) for axis, length in enumerate(array.shape)]
    main_axis = array.shape.index(max(array.shape))
    neighbour = place[:main_axis] + [(place[main_axis] + 1) % array.shape[main_axis]] + place[main_axis + 1:]
    return array.at[tuple(place)].set(low).at[tuple(neighbour)].set(high)


def setup_inputs(seed: int = 0, part: int = 0) -> dict:
    key_of = jax.random.split(jax.random.key(seed), 6)
    part_splits = jax.random.split(jax.random.fold_in(key_of[5], part), 6)
    template = draw_template(jax.random.fold_in(jax.random.fold_in(key_of[5], part), 71), part)
    science = draw_science(jax.random.fold_in(jax.random.fold_in(key_of[5], part), 71), part)
    flags = plant((jax.random.randint(part_splits[2], (EPOCHS, ROWS, COLS), 0, 16) < 1).astype(jnp.int32), jax.random.fold_in(part_splits[2], 1), 0, 1)
    stamp_rows = plant(jax.random.randint(part_splits[3], (EPOCHS, STAMPS), 0, R_DEV - STAMP + 1), jax.random.fold_in(part_splits[3], 1), 0, R_DEV - STAMP).astype(jnp.int32)
    stamp_cols = plant(jax.random.randint(part_splits[4], (EPOCHS, STAMPS), 0, COLS - STAMP + 1), jax.random.fold_in(part_splits[4], 1), 0, COLS - STAMP).astype(jnp.int32)
    return dict(template=template, science=science, flags=flags, stamp_rows=stamp_rows, stamp_cols=stamp_cols)


def basis_profiles():
    offsets = jnp.arange(15, dtype=jnp.float32) - 7.0
    row_list = []
    col_list = []
    for sigma in (1.0, 2.0, 3.5):
        gauss = jnp.exp(-offsets * offsets / (2.0 * sigma * sigma))
        gauss = gauss / jnp.sum(gauss)
        for power_r, power_c in ((0, 0), (1, 0), (0, 1), (1, 1)):
            row_list.append(gauss * (offsets / 7.0) if power_r else gauss)
            col_list.append(gauss * (offsets / 7.0) if power_c else gauss)
    return (jnp.stack(row_list), jnp.stack(col_list))

def psf_profile():
    offsets = jnp.arange(15, dtype=jnp.float32) - 7.0
    gauss = jnp.exp(-offsets * offsets / 4.5)
    return (gauss / jnp.sum(gauss))[None, :]

def conv_rows(extended, profile):
    count = extended.shape[0] - 14
    total = jnp.zeros((profile.shape[0], count, extended.shape[1]), jnp.float32)
    for shift in range(15):
        total = total + profile[:, shift, None, None] * extended[None, shift:shift + count, :]
    return total

def conv_cols(extended, profile):
    count = extended.shape[2] - 14
    total = jnp.zeros((profile.shape[0], extended.shape[1], count), jnp.float32)
    for shift in range(15):
        total = total + profile[:, shift, None, None] * extended[:, :, shift:shift + count]
    return total

def reference(template, science, flags, stamp_rows, stamp_cols):
    row_prof, col_prof = basis_profiles()
    images = conv_cols(conv_rows(jnp.pad(template, 7), row_prof), col_prof)
    tile_of = (jnp.arange(stamp_rows.shape[1]) // STAMPS_DEV).astype(jnp.int32)
    top = stamp_rows + tile_of[None, :] * R_DEV
    pos_r = jnp.arange(ROWS).astype(jnp.int32)
    pos_c = jnp.arange(COLS).astype(jnp.int32)

    def one_epoch(epoch):
        row_ind = ((pos_r[None, :] >= top[epoch][:, None]) & (pos_r[None, :] < top[epoch][:, None] + STAMP)).astype(jnp.float32)
        col_ind = ((pos_c[None, :] >= stamp_cols[epoch][:, None]) & (pos_c[None, :] < stamp_cols[epoch][:, None] + STAMP)).astype(jnp.float32)
        weight = jnp.dot(row_ind.T, col_ind, precision=lax.Precision.HIGHEST)
        good = jnp.where(flags[epoch] == 0, weight, 0.0)
        normal = jnp.einsum('kpq,lpq->kl', images * good[None], images, precision=lax.Precision.HIGHEST)
        rhs = jnp.einsum('kpq,pq->k', images, good * science[epoch], precision=lax.Precision.HIGHEST)
        return (normal, rhs)
    normals, rhss = lax.map(one_epoch, jnp.arange(science.shape[0]).astype(jnp.int32))
    normal = jnp.sum(normals, axis=0)
    rhs = jnp.sum(rhss, axis=0)
    system = normal + 0.05 * jnp.trace(normal) / NBASIS * jnp.eye(NBASIS, dtype=jnp.float32)
    coefficients = jnp.linalg.solve(system, rhs)
    model = jnp.einsum('k,kpq->pq', coefficients, images, precision=lax.Precision.HIGHEST)
    psf = psf_profile()

    def filter_one(epoch):
        difference = science[epoch] - model
        return conv_cols(conv_rows(jnp.pad(difference, 7), psf), psf)[0]
    detection = lax.map(filter_one, jnp.arange(science.shape[0]).astype(jnp.int32))
    return (detection, coefficients)
```

```python
import functools
import math

import jax
import jax.numpy as jnp
from jax import lax
from jax.experimental import pallas as pl
from jax.experimental.pallas import tpu as pltpu
from jax.sharding import PartitionSpec as P

STAMP = 32
HALF = 7
SIGMAS = (1.0, 2.0, 3.5)
PSF = 1.5
RH = 16
DH = 8
PAD = 64
F32 = jnp.float32
BF16 = jnp.bfloat16
HIGHEST = lax.Precision.HIGHEST


def norm_of(sigma):
    return sum(math.exp(-o * o / (2.0 * sigma * sigma)) for o in range(-HALF, HALF + 1))


def gauss_of(offset, sigma, where=None):
    keep = jnp.abs(offset) <= HALF
    if where is not None:
        keep = keep & where
    value = jnp.exp(offset * offset * (-1.0 / (2.0 * sigma * sigma))) * (1.0 / norm_of(sigma))
    return jnp.where(keep, value, 0.0)


def band_offset(rows, cols, axis, shift):
    r = lax.broadcasted_iota(jnp.int32, (rows, cols), 0)
    c = lax.broadcasted_iota(jnp.int32, (rows, cols), 1)
    delta = (c - r) if axis == 1 else (r - c)
    return (delta - shift).astype(F32)


def split(x):
    hi = x.astype(BF16)
    return hi, (x - hi.astype(F32)).astype(BF16)


def mm(a, b):
    return jnp.dot(a, b, preferred_element_type=F32)


def mm3(a, b):
    return mm(a[0], b[0]) + mm(a[1], b[0]) + mm(a[0], b[1])


def fill_padded(ext_ref, tpad):
    count, rows, width = ext_ref.shape
    total = count * width
    tpad[:, :PAD] = jnp.zeros((rows, PAD), F32)
    tpad[:, PAD + total :] = jnp.zeros((rows, tpad.shape[1] - PAD - total), F32)
    for e in range(count):
        tpad[:, PAD + e * width : PAD + (e + 1) * width] = ext_ref[e]


def stamp_kernel(top_ref, left_ref, ext_ref, sci_ref, flag_ref, out_ref, tpad, tst, sst, gst, acc):
    stamps = top_ref.shape[1]
    cols = sci_ref.shape[1]
    fill_padded(ext_ref, tpad)
    lane = lax.broadcasted_iota(jnp.int32, (1, 128), 1)
    for s in range(stamps):
        top = top_ref[0, s]
        left = left_ref[0, s]
        start = left + (PAD - HALF)
        base = jnp.minimum(start // 128 * 128, tpad.shape[1] - 256)
        level = top // 8 * 8
        win = tpad[pl.ds(pl.multiple_of(level + DH, 8), 56), pl.ds(pl.multiple_of(base, 128), 256)]
        slot = 64 * (s % 2)
        moved = pltpu.roll(win, lax.rem(slot - (start - base) + 512, 256), 1)[:, :128]
        moved = pltpu.roll(moved, lax.rem(level - top + 56, 56), 0)[:48]
        at = pl.ds(128 * (s // 2), 128)
        if s % 2 == 0:
            tst[:, at] = moved
        else:
            tst[:, at] = jnp.where(lane >= 64, moved, tst[:, at])
        base = jnp.minimum(left // 128 * 128, cols - 256)
        slot = 32 * (s % 4)
        shift = lax.rem(slot - (left - base) + 512, 256)
        level = jnp.minimum(level, sci_ref.shape[0] - 40)
        back = lax.rem(level - top + 40, 40)
        where = (pl.ds(pl.multiple_of(level, 8), 40), pl.ds(pl.multiple_of(base, 128), 256))
        sci = pltpu.roll(sci_ref[where], shift, 1)[:, :128]
        sci = pltpu.roll(sci, back, 0)[:STAMP]
        good = jnp.where(flag_ref[where] == 0, 1.0, 0.0).astype(F32)
        good = pltpu.roll(good, shift, 1)[:, :128]
        good = pltpu.roll(good, back, 0)[:STAMP]
        at = pl.ds(STAMP * (s // 4), STAMP)
        if s % 4 == 0:
            sst[at, :] = sci
            gst[at, :] = good
        else:
            sst[at, :] = jnp.where(lane >= slot, sci, sst[at, :])
            gst[at, :] = jnp.where(lane >= slot, good, gst[at, :])
    offset = band_offset(STAMP, 48, 1, DH)
    parts = []
    for sigma in SIGMAS:
        g = gauss_of(offset, sigma)
        parts += [g, g * (offset * (1.0 / HALF))]
    rows = mm3(split(jnp.concatenate(parts, axis=0)), split(tst[...]))
    quads = stamps // 4
    r = lax.broadcasted_iota(jnp.int32, (256, 128), 0)
    c = lax.broadcasted_iota(jnp.int32, (256, 128), 1)
    same = (r // 64) == (c // STAMP)
    offset = ((r % 64) - (c % STAMP) - HALF).astype(F32)
    images = [None] * 12
    for k, sigma in enumerate(SIGMAS):
        lhs = split(
            jnp.concatenate(
                [rows[64 * k : 64 * k + 64, 256 * q : 256 * q + 256] for q in range(quads)], axis=0
            )
        )
        g = gauss_of(offset, sigma, same)
        for j in range(2):
            out = mm3(lhs, split(g * (offset * (1.0 / HALF)) if j else g))
            for i in range(2):
                images[4 * k + i + 2 * j] = jnp.concatenate(
                    [out[64 * q + 32 * i : 64 * q + 32 * i + 32] for q in range(quads)], axis=0
                )
    acc[...] = jnp.zeros_like(acc)
    good = gst[...]
    sci = sst[...]
    for k in range(12):
        weighted = images[k] * good
        acc[16 * k + 12 : 16 * k + 13, :] = jnp.sum(weighted * sci, axis=0, keepdims=True)
        for l in range(k + 1):
            value = jnp.sum(weighted * images[l], axis=0, keepdims=True)
            acc[16 * k + l : 16 * k + l + 1, :] = value
            if l < k:
                acc[16 * l + k : 16 * l + k + 1, :] = value
    n = acc.shape[0]
    summed = jnp.dot(acc[...], jnp.ones((128, 128), F32), precision=HIGHEST)
    r = lax.broadcasted_iota(jnp.int32, (n, 128), 0)
    c = lax.broadcasted_iota(jnp.int32, (n, 128), 1)
    summed = jnp.where(r % 16 == c, summed, 0.0)
    r = lax.broadcasted_iota(jnp.int32, (16, n), 0)
    c = lax.broadcasted_iota(jnp.int32, (16, n), 1)
    pick = jnp.where(c // 16 == r, 1.0, 0.0).astype(F32)
    out_ref[...] = jnp.dot(pick, summed, precision=HIGHEST)


def solve_system(system):
    r = lax.broadcasted_iota(jnp.int32, (16, 128), 0)
    c = lax.broadcasted_iota(jnp.int32, (16, 128), 1)
    diag = (r == c) & (r < 12)
    trace = jnp.sum(jnp.where(diag, system, 0.0), keepdims=True)
    m = system + jnp.where(diag, 0.05 * trace / 12.0, 0.0)
    for p in range(12):
        row = m[p : p + 1, :] / m[p : p + 1, p : p + 1]
        m = jnp.where(r == p, row, m - m[:, p : p + 1] * row)
    return m


def final_kernel(tiles, sys_ref, ext_ref, halo_ref, sci_ref, det_ref, coef_ref, tpad, phi, plo, dpad, ahi, alo):
    rows, cols = sci_ref.shape
    drows = rows + 2 * DH
    half = drows // 2 // 16 * 16
    rest = drows - half
    taps = rest + 2 * DH
    fill_padded(ext_ref, tpad)
    offset = band_offset(rest, taps, 1, DH)
    for k, sigma in enumerate(SIGMAS):
        g = gauss_of(offset, sigma)
        for i in range(2):
            ahi[2 * k + i], alo[2 * k + i] = split(g * (offset * (1.0 / HALF)) if i else g)
    for b in range(2):
        src = split(tpad[b * half : b * half + taps, :])
        keep = half if b == 0 else rest

        def one(s, _, src=src, b=b, keep=keep):
            hi, lo = split(mm3((ahi[s], alo[s]), src))
            phi[s, b * half : b * half + keep, :] = hi[:keep]
            plo[s, b * half : b * half + keep, :] = lo[:keep]
            return _

        lax.fori_loop(0, 6, one, 0)
    solved = solve_system(sys_ref[...])
    r = lax.broadcasted_iota(jnp.int32, (16, 128), 0)
    c = lax.broadcasted_iota(jnp.int32, (16, 128), 1)
    coef = jnp.sum(jnp.where(r == c, solved[:, 12:13], 0.0), axis=0, keepdims=True)
    coef_ref[...] = coef[:, :12]
    offset = band_offset(256 + 2 * PAD, 256, 0, PAD)
    scaled = offset * (1.0 / HALF)
    mats = []
    for k, sigma in enumerate(SIGMAS):
        g = gauss_of(offset, sigma)
        for i in range(2):
            a = solved[4 * k + i : 4 * k + i + 1, 12:13]
            b = solved[4 * k + i + 2 : 4 * k + i + 3, 12:13]
            mats.append(split(g * (a + b * scaled)))
    dpad[:, :PAD] = jnp.zeros((drows, PAD), F32)
    dpad[:, PAD + cols :] = jnp.zeros((drows, PAD), F32)
    tile = lax.axis_index("tile")
    r = lax.broadcasted_iota(jnp.int32, (DH, 1), 0)
    above = jnp.where(tile > 0, 1.0, 0.0).astype(F32)
    below = jnp.where(tile < tiles - 1, 1.0, 0.0).astype(F32)
    for j in range(cols // 256):
        at = slice(256 * j, 256 * j + 256 + 2 * PAD)
        model = jnp.zeros((drows, 256), F32)
        for s in range(6):
            model = model + mm3((phi[s, :, at], plo[s, :, at]), mats[s])
        here = slice(256 * j, 256 * j + 256)
        to = slice(PAD + 256 * j, PAD + 256 * j + 256)
        dpad[:DH, to] = (halo_ref[:DH, here] - model[:DH]) * above
        dpad[DH : DH + rows, to] = sci_ref[:, here] - model[DH : DH + rows]
        dpad[DH + rows :, to] = (halo_ref[DH:, here] - model[DH + rows :]) * below
    psf_row = split(gauss_of(band_offset(128, 128 + 2 * DH, 1, DH), PSF))
    psf_col = split(gauss_of(offset, PSF))
    for b in range(rows // 128):
        inner = mm3(psf_row, split(dpad[128 * b : 128 * b + 128 + 2 * DH, :]))
        hi, lo = split(inner)
        for j in range(cols // 256):
            at = slice(256 * j, 256 * j + 256 + 2 * PAD)
            det_ref[128 * b : 128 * b + 128, 256 * j : 256 * j + 256] = mm3(
                (hi[:, at], lo[:, at]), psf_col
            )


def exchange(block, width, tiles):
    down = [(i, i + 1) for i in range(tiles - 1)]
    up = [(b, a) for a, b in down]
    low = lax.ppermute(block[-width:], "tile", down)
    high = lax.ppermute(block[:width], "tile", up)
    return low, high


def vmem_specs(count):
    return [pl.BlockSpec(memory_space=pltpu.VMEM)] * count


def local(tiles, template, science, flags, stamp_rows, stamp_cols):
    low, high = exchange(template, RH, tiles)
    own = jnp.concatenate([low, template, high], axis=0)
    ext = lax.all_gather(own, "epoch", axis=0, tiled=False)
    low, high = exchange(science[0], DH, tiles)
    halo = jnp.concatenate([low, high], axis=0)
    sci = science[0]
    rows, cols = sci.shape
    ext_rows = rows + 2 * RH
    padded = cols + 2 * PAD
    stamps = stamp_rows.shape[1]
    partial = pl.pallas_call(
        stamp_kernel,
        out_shape=jax.ShapeDtypeStruct((16, 128), F32),
        in_specs=[pl.BlockSpec(memory_space=pltpu.SMEM)] * 2 + vmem_specs(3),
        out_specs=pl.BlockSpec(memory_space=pltpu.VMEM),
        scratch_shapes=[
            pltpu.VMEM((ext_rows, padded), F32),
            pltpu.VMEM((48, 64 * stamps), F32),
            pltpu.VMEM((STAMP * stamps // 4, 128), F32),
            pltpu.VMEM((STAMP * stamps // 4, 128), F32),
            pltpu.VMEM((192, 128), F32),
        ],
        name="stamps",
    )(stamp_rows, stamp_cols, ext, sci, flags[0])
    system = lax.psum(partial, ("epoch", "tile"))
    drows = rows + 2 * DH
    rest = drows - drows // 2 // 16 * 16
    detection, coefficients = pl.pallas_call(
        functools.partial(final_kernel, tiles),
        out_shape=(
            jax.ShapeDtypeStruct((rows, cols), F32),
            jax.ShapeDtypeStruct((1, 12), F32),
        ),
        in_specs=vmem_specs(4),
        out_specs=tuple(vmem_specs(2)),
        scratch_shapes=[
            pltpu.VMEM((ext_rows, padded), F32),
            pltpu.VMEM((6, drows, padded), BF16),
            pltpu.VMEM((6, drows, padded), BF16),
            pltpu.VMEM((drows, padded), F32),
            pltpu.VMEM((6, rest, rest + 2 * DH), BF16),
            pltpu.VMEM((6, rest, rest + 2 * DH), BF16),
        ],
        compiler_params=pltpu.CompilerParams(vmem_limit_bytes=48 * 1024 * 1024),
        name="final",
    )(system, ext, halo, sci)
    return (detection[None], coefficients.reshape(12))


def solution(mesh):
    return jax.shard_map(
        functools.partial(local, mesh.shape["tile"]),
        mesh=mesh,
        in_specs=(
            P(("patch", "tile"), "epoch"),
            P(("patch", "epoch"), "tile", None),
            P(("patch", "epoch"), "tile", None),
            P(("patch", "epoch"), "tile"),
            P(("patch", "epoch"), "tile"),
        ),
        out_specs=(P(("patch", "epoch"), "tile", None), P("patch")),
        check_vma=False,
    )
```

```python
import functools
import math

import jax
import jax.numpy as jnp
from jax import lax
from jax.experimental import pallas as pl
from jax.experimental.pallas import tpu as pltpu
from jax.sharding import PartitionSpec as P

STAMP = 32
HALF = 7
SIGMAS = (1.0, 2.0, 3.5)
PSF = 1.5
RH = 16
DH = 8
PAD = 64
F32 = jnp.float32
BF16 = jnp.bfloat16
HIGHEST = lax.Precision.HIGHEST
MESH = pl.DeviceIdType.MESH
CHUNKS = 4


def norm_of(sigma):
    return sum(math.exp(-o * o / (2.0 * sigma * sigma)) for o in range(-HALF, HALF + 1))


def gauss_of(offset, sigma, where=None):
    keep = jnp.abs(offset) <= HALF
    if where is not None:
        keep = keep & where
    value = jnp.exp(offset * offset * (-1.0 / (2.0 * sigma * sigma))) * (1.0 / norm_of(sigma))
    return jnp.where(keep, value, 0.0)


def band_offset(rows, cols, axis, shift):
    r = lax.broadcasted_iota(jnp.int32, (rows, cols), 0)
    c = lax.broadcasted_iota(jnp.int32, (rows, cols), 1)
    delta = (c - r) if axis == 1 else (r - c)
    return (delta - shift).astype(F32)


def split(x):
    hi = x.astype(BF16)
    return hi, (x - hi.astype(F32)).astype(BF16)


def mm(a, b):
    return jnp.dot(a, b, preferred_element_type=F32)


def mm3(a, b):
    return mm(a[0], b[0]) + mm(a[1], b[0]) + mm(a[0], b[1])


def inner_edges(tiles):
    tile = lax.axis_index("tile")
    above = jnp.where(tile > 0, 1.0, 0.0).astype(F32)
    below = jnp.where(tile < tiles - 1, 1.0, 0.0).astype(F32)
    return above, below


def fill_padded(tiles, blocks_ref, edges_ref, tpad):
    count, rows, width = blocks_ref.shape
    total = count * width
    above, below = inner_edges(tiles)
    tpad[:, :PAD] = jnp.zeros((tpad.shape[0], PAD), F32)
    tpad[:, PAD + total :] = jnp.zeros((tpad.shape[0], tpad.shape[1] - PAD - total), F32)
    for e in range(count):
        at = slice(PAD + e * width, PAD + (e + 1) * width)
        tpad[RH : RH + rows, at] = blocks_ref[e]
        tpad[:RH, at] = edges_ref[e] * above
        tpad[RH + rows :, at] = edges_ref[e] * below


def stamp_kernel(tiles, top_ref, left_ref, blocks_ref, edges_ref, sci_ref, flag_ref, out_ref, tpad, tst, sst, gst, acc):
    stamps = top_ref.shape[1]
    cols = sci_ref.shape[1]
    fill_padded(tiles, blocks_ref, edges_ref, tpad)
    lane = lax.broadcasted_iota(jnp.int32, (1, 128), 1)
    for s in range(stamps):
        top = top_ref[0, s]
        left = left_ref[0, s]
        start = left + (PAD - HALF)
        base = jnp.minimum(start // 128 * 128, tpad.shape[1] - 256)
        level = top // 8 * 8
        win = tpad[pl.ds(pl.multiple_of(level + DH, 8), 56), pl.ds(pl.multiple_of(base, 128), 256)]
        slot = 64 * (s % 2)
        moved = pltpu.roll(win, lax.rem(slot - (start - base) + 512, 256), 1)[:, :128]
        moved = pltpu.roll(moved, lax.rem(level - top + 56, 56), 0)[:48]
        at = pl.ds(128 * (s // 2), 128)
        if s % 2 == 0:
            tst[:, at] = moved
        else:
            tst[:, at] = jnp.where(lane >= 64, moved, tst[:, at])
        base = jnp.minimum(left // 128 * 128, cols - 256)
        slot = 32 * (s % 4)
        shift = lax.rem(slot - (left - base) + 512, 256)
        level = jnp.minimum(level, sci_ref.shape[0] - 40)
        back = lax.rem(level - top + 40, 40)
        where = (pl.ds(pl.multiple_of(level, 8), 40), pl.ds(pl.multiple_of(base, 128), 256))
        sci = pltpu.roll(sci_ref[where], shift, 1)[:, :128]
        sci = pltpu.roll(sci, back, 0)[:STAMP]
        good = jnp.where(flag_ref[where] == 0, 1.0, 0.0).astype(F32)
        good = pltpu.roll(good, shift, 1)[:, :128]
        good = pltpu.roll(good, back, 0)[:STAMP]
        at = pl.ds(STAMP * (s // 4), STAMP)
        if s % 4 == 0:
            sst[at, :] = sci
            gst[at, :] = good
        else:
            sst[at, :] = jnp.where(lane >= slot, sci, sst[at, :])
            gst[at, :] = jnp.where(lane >= slot, good, gst[at, :])
    offset = band_offset(STAMP, 48, 1, DH)
    parts = []
    for sigma in SIGMAS:
        g = gauss_of(offset, sigma)
        parts += [g, g * (offset * (1.0 / HALF))]
    rows = mm3(split(jnp.concatenate(parts, axis=0)), split(tst[...]))
    quads = stamps // 4
    r = lax.broadcasted_iota(jnp.int32, (256, 128), 0)
    c = lax.broadcasted_iota(jnp.int32, (256, 128), 1)
    same = (r // 64) == (c // STAMP)
    offset = ((r % 64) - (c % STAMP) - HALF).astype(F32)
    images = [None] * 12
    for k, sigma in enumerate(SIGMAS):
        lhs = split(
            jnp.concatenate(
                [rows[64 * k : 64 * k + 64, 256 * q : 256 * q + 256] for q in range(quads)], axis=0
            )
        )
        g = gauss_of(offset, sigma, same)
        for j in range(2):
            out = mm3(lhs, split(g * (offset * (1.0 / HALF)) if j else g))
            for i in range(2):
                images[4 * k + i + 2 * j] = jnp.concatenate(
                    [out[64 * q + 32 * i : 64 * q + 32 * i + 32] for q in range(quads)], axis=0
                )
    acc[...] = jnp.zeros_like(acc)
    good = gst[...]
    sci = sst[...]
    for k in range(12):
        weighted = images[k] * good
        acc[16 * k + 12 : 16 * k + 13, :] = jnp.sum(weighted * sci, axis=0, keepdims=True)
        for l in range(k + 1):
            value = jnp.sum(weighted * images[l], axis=0, keepdims=True)
            acc[16 * k + l : 16 * k + l + 1, :] = value
            if l < k:
                acc[16 * l + k : 16 * l + k + 1, :] = value
    n = acc.shape[0]
    summed = jnp.dot(acc[...], jnp.ones((128, 128), F32), precision=HIGHEST)
    r = lax.broadcasted_iota(jnp.int32, (n, 128), 0)
    c = lax.broadcasted_iota(jnp.int32, (n, 128), 1)
    summed = jnp.where(r % 16 == c, summed, 0.0)
    r = lax.broadcasted_iota(jnp.int32, (16, n), 0)
    c = lax.broadcasted_iota(jnp.int32, (16, n), 1)
    pick = jnp.where(c // 16 == r, 1.0, 0.0).astype(F32)
    out_ref[...] = jnp.dot(pick, summed, precision=HIGHEST)


def solve_system(system):
    r = lax.broadcasted_iota(jnp.int32, (16, 128), 0)
    c = lax.broadcasted_iota(jnp.int32, (16, 128), 1)
    diag = (r == c) & (r < 12)
    trace = jnp.sum(jnp.where(diag, system, 0.0), keepdims=True)
    m = system + jnp.where(diag, 0.05 * trace / 12.0, 0.0)
    for p in range(12):
        row = m[p : p + 1, :] / m[p : p + 1, p : p + 1]
        m = jnp.where(r == p, row, m - m[:, p : p + 1] * row)
    return m


def final_kernel(tiles, sys_ref, blocks_ref, edges_ref, halo_ref, sci_ref, det_ref, coef_ref, tpad, phi, plo, dpad, ahi, alo):
    rows, cols = sci_ref.shape
    drows = rows + 2 * DH
    half = drows // 2 // 16 * 16
    rest = drows - half
    taps = rest + 2 * DH
    fill_padded(tiles, blocks_ref, edges_ref, tpad)
    offset = band_offset(rest, taps, 1, DH)
    for k, sigma in enumerate(SIGMAS):
        g = gauss_of(offset, sigma)
        for i in range(2):
            ahi[2 * k + i], alo[2 * k + i] = split(g * (offset * (1.0 / HALF)) if i else g)
    for b in range(2):
        src = split(tpad[b * half : b * half + taps, :])
        keep = half if b == 0 else rest

        def one(s, _, src=src, b=b, keep=keep):
            hi, lo = split(mm3((ahi[s], alo[s]), src))
            phi[s, b * half : b * half + keep, :] = hi[:keep]
            plo[s, b * half : b * half + keep, :] = lo[:keep]
            return _

        lax.fori_loop(0, 6, one, 0)
    solved = solve_system(sys_ref[...])
    r = lax.broadcasted_iota(jnp.int32, (16, 128), 0)
    c = lax.broadcasted_iota(jnp.int32, (16, 128), 1)
    coef = jnp.sum(jnp.where(r == c, solved[:, 12:13], 0.0), axis=0, keepdims=True)
    coef_ref[...] = coef[:, :12]
    offset = band_offset(256 + 2 * PAD, 256, 0, PAD)
    scaled = offset * (1.0 / HALF)
    mats = []
    for k, sigma in enumerate(SIGMAS):
        g = gauss_of(offset, sigma)
        for i in range(2):
            a = solved[4 * k + i : 4 * k + i + 1, 12:13]
            b = solved[4 * k + i + 2 : 4 * k + i + 3, 12:13]
            mats.append(split(g * (a + b * scaled)))
    dpad[:, :PAD] = jnp.zeros((drows, PAD), F32)
    dpad[:, PAD + cols :] = jnp.zeros((drows, PAD), F32)
    above, below = inner_edges(tiles)
    for j in range(cols // 256):
        at = slice(256 * j, 256 * j + 256 + 2 * PAD)
        model = jnp.zeros((drows, 256), F32)
        for s in range(6):
            model = model + mm3((phi[s, :, at], plo[s, :, at]), mats[s])
        here = slice(256 * j, 256 * j + 256)
        to = slice(PAD + 256 * j, PAD + 256 * j + 256)
        dpad[:DH, to] = (halo_ref[:, here] - model[:DH]) * above
        dpad[DH : DH + rows, to] = sci_ref[:, here] - model[DH : DH + rows]
        dpad[DH + rows :, to] = (halo_ref[:, here] - model[DH + rows :]) * below
    psf_row = split(gauss_of(band_offset(128, 128 + 2 * DH, 1, DH), PSF))
    psf_col = split(gauss_of(offset, PSF))
    for b in range(rows // 128):
        inner = mm3(psf_row, split(dpad[128 * b : 128 * b + 128 + 2 * DH, :]))
        hi, lo = split(inner)
        for j in range(cols // 256):
            at = slice(256 * j, 256 * j + 256 + 2 * PAD)
            det_ref[128 * b : 128 * b + 128, 256 * j : 256 * j + 256] = mm3(
                (hi[:, at], lo[:, at]), psf_col
            )


def ring_place(count, paired):
    if not paired:
        return lambda e: e, lambda p: p
    half = count // 2

    def position(e):
        z, y = e // 2, e % 2
        return z + y * (count - 1 - 2 * z)

    def index(p):
        far = p // half
        return 2 * p * (1 - far) + far * (2 * (count - 1 - p) + 1)

    return position, index


def gather_kernel(count, paired, own_ref, sci_ref, blocks, edges, halo, ssem, rsem, esend, erecv, hsem, lsem):
    me = lax.axis_index("epoch")
    tile = lax.axis_index("tile")
    position, index = ring_place(count, paired)
    pos = position(me)
    ring = (index(lax.rem(pos + 1, count)), index(lax.rem(pos + count - 1, count)))
    other = 1 - tile
    barrier = pltpu.get_barrier_semaphore()
    for e in ring:
        pl.semaphore_signal(barrier, inc=1, device_id={"epoch": e}, device_id_type=MESH)
    pl.semaphore_signal(barrier, inc=1, device_id={"tile": other}, device_id_type=MESH)
    keep = pltpu.make_async_copy(own_ref, blocks.at[me], lsem)
    keep.start()
    pl.semaphore_wait(barrier, 3)
    rows = own_ref.shape[0]
    chunk = rows // CHUNKS

    def move(way, step, c, origin, src=None):
        at = pl.ds(c * chunk, chunk)
        return pltpu.make_async_remote_copy(
            src_ref=blocks.at[origin, at] if src is None else src.at[at],
            dst_ref=blocks.at[origin, at],
            send_sem=ssem.at[way, step, c],
            recv_sem=rsem.at[way, step, c],
            device_id={"epoch": ring[way]},
            device_id_type=MESH,
        )

    def edge(step, origin, src=None):
        at = pl.ds(pl.multiple_of(other * (rows - RH), 8), RH)
        return pltpu.make_async_remote_copy(
            src_ref=blocks.at[origin, at] if src is None else src.at[at],
            dst_ref=edges.at[origin],
            send_sem=esend.at[step],
            recv_sem=erecv.at[step],
            device_id={"tile": other},
            device_id_type=MESH,
        )

    reach = (count // 2, count - 1 - count // 2)
    started = []
    for c in range(CHUNKS):
        for way in range(2):
            if reach[way]:
                started.append(move(way, 0, c, me, own_ref))
                started[-1].start()
    first = edge(0, me, own_ref)
    first.start()
    at = pl.ds(pl.multiple_of(other * (sci_ref.shape[0] - DH), 8), DH)
    science = pltpu.make_async_remote_copy(
        src_ref=sci_ref.at[at],
        dst_ref=halo,
        send_sem=hsem.at[0],
        recv_sem=hsem.at[1],
        device_id={"tile": other},
        device_id_type=MESH,
    )
    science.start()
    side = [first]
    taken = 1
    for step in range(1, reach[0] + 1):
        for c in range(CHUNKS):
            for way in range(2):
                if step > reach[way]:
                    continue
                back = pos + (count - step if way == 0 else step)
                origin = index(lax.rem(back, count))
                move(way, step - 1, c, origin).wait_recv()
                if step < reach[way]:
                    started.append(move(way, step, c, origin))
                    started[-1].start()
                if c == CHUNKS - 1:
                    side.append(edge(taken, origin))
                    side[-1].start()
                    taken += 1
    for copy in started:
        copy.wait_send()
    for copy in side:
        copy.wait()
    science.wait()
    keep.wait()


def sum_kernel(epochs, tiles, part_ref, out_ref, slots, ssem, rsem, lsem):
    count = epochs * tiles
    me = lax.axis_index("epoch") * tiles + lax.axis_index("tile")
    barrier = pltpu.get_barrier_semaphore()

    def where(d):
        peer = lax.rem(me + d, count)
        return {"epoch": peer // tiles, "tile": peer % tiles}

    def greet(d, _):
        pl.semaphore_signal(barrier, inc=1, device_id=where(d), device_id_type=MESH)
        return _

    lax.fori_loop(1, count, greet, 0)
    keep = pltpu.make_async_copy(part_ref, slots.at[me], lsem)
    keep.start()
    pl.semaphore_wait(barrier, count - 1)

    def copy(d, slot):
        return pltpu.make_async_remote_copy(
            src_ref=part_ref,
            dst_ref=slots.at[slot],
            send_sem=ssem.at[d],
            recv_sem=rsem.at[d],
            device_id=where(d),
            device_id_type=MESH,
        )

    def send(d, _):
        copy(d, me).start()
        return _

    lax.fori_loop(1, count, send, 0)
    keep.wait()

    def finish(d, _):
        made = copy(d, lax.rem(me + count - d, count))
        made.wait_send()
        made.wait_recv()
        return _

    lax.fori_loop(1, count, finish, 0)
    out_ref[...] = jnp.sum(slots[...], axis=0)


def vmem_specs(count):
    return [pl.BlockSpec(memory_space=pltpu.VMEM)] * count


def local(epochs, tiles, paired, template, science, flags, stamp_rows, stamp_cols):
    sci = science[0]
    rows, cols = sci.shape
    width = template.shape[1]
    ext_rows = rows + 2 * RH
    padded = cols + 2 * PAD
    stamps = stamp_rows.shape[1]
    reach = epochs // 2
    blocks, edges, halo = pl.pallas_call(
        functools.partial(gather_kernel, epochs, paired),
        out_shape=(
            jax.ShapeDtypeStruct((epochs, rows, width), F32),
            jax.ShapeDtypeStruct((epochs, RH, width), F32),
            jax.ShapeDtypeStruct((DH, cols), F32),
        ),
        in_specs=vmem_specs(2),
        out_specs=tuple(vmem_specs(3)),
        scratch_shapes=[
            pltpu.SemaphoreType.DMA((2, reach, CHUNKS)),
            pltpu.SemaphoreType.DMA((2, reach, CHUNKS)),
            pltpu.SemaphoreType.DMA((epochs,)),
            pltpu.SemaphoreType.DMA((epochs,)),
            pltpu.SemaphoreType.DMA((2,)),
            pltpu.SemaphoreType.DMA,
        ],
        compiler_params=pltpu.CompilerParams(collective_id=0, has_side_effects=True),
        name="gather",
    )(template, sci)
    partial = pl.pallas_call(
        functools.partial(stamp_kernel, tiles),
        out_shape=jax.ShapeDtypeStruct((16, 128), F32),
        in_specs=[pl.BlockSpec(memory_space=pltpu.SMEM)] * 2 + vmem_specs(4),
        out_specs=pl.BlockSpec(memory_space=pltpu.VMEM),
        scratch_shapes=[
            pltpu.VMEM((ext_rows, padded), F32),
            pltpu.VMEM((48, 64 * stamps), F32),
            pltpu.VMEM((STAMP * stamps // 4, 128), F32),
            pltpu.VMEM((STAMP * stamps // 4, 128), F32),
            pltpu.VMEM((192, 128), F32),
        ],
        name="stamps",
    )(stamp_rows, stamp_cols, blocks, edges, sci, flags[0])
    system = pl.pallas_call(
        functools.partial(sum_kernel, epochs, tiles),
        out_shape=jax.ShapeDtypeStruct((16, 128), F32),
        in_specs=vmem_specs(1),
        out_specs=pl.BlockSpec(memory_space=pltpu.VMEM),
        scratch_shapes=[
            pltpu.VMEM((epochs * tiles, 16, 128), F32),
            pltpu.SemaphoreType.DMA((epochs * tiles,)),
            pltpu.SemaphoreType.DMA((epochs * tiles,)),
            pltpu.SemaphoreType.DMA,
        ],
        compiler_params=pltpu.CompilerParams(collective_id=1, has_side_effects=True),
        name="total",
    )(partial)
    drows = rows + 2 * DH
    rest = drows - drows // 2 // 16 * 16
    detection, coefficients = pl.pallas_call(
        functools.partial(final_kernel, tiles),
        out_shape=(
            jax.ShapeDtypeStruct((rows, cols), F32),
            jax.ShapeDtypeStruct((1, 12), F32),
        ),
        in_specs=vmem_specs(5),
        out_specs=tuple(vmem_specs(2)),
        scratch_shapes=[
            pltpu.VMEM((ext_rows, padded), F32),
            pltpu.VMEM((6, drows, padded), BF16),
            pltpu.VMEM((6, drows, padded), BF16),
            pltpu.VMEM((drows, padded), F32),
            pltpu.VMEM((6, rest, rest + 2 * DH), BF16),
            pltpu.VMEM((6, rest, rest + 2 * DH), BF16),
        ],
        compiler_params=pltpu.CompilerParams(vmem_limit_bytes=48 * 1024 * 1024),
        name="final",
    )(system, blocks, edges, halo, sci)
    return (detection[None], coefficients.reshape(12))


def solution(mesh):
    line = mesh.devices[0, :, 0]
    columns = {tuple(getattr(d, "coords", (0, 0)))[:2] for d in line}
    paired = len(columns) == 2 and len(line) % 2 == 0
    return jax.shard_map(
        functools.partial(local, mesh.shape["epoch"], mesh.shape["tile"], paired),
        mesh=mesh,
        in_specs=(
            P(("patch", "tile"), "epoch"),
            P(("patch", "epoch"), "tile", None),
            P(("patch", "epoch"), "tile", None),
            P(("patch", "epoch"), "tile"),
            P(("patch", "epoch"), "tile"),
        ),
        out_specs=(P(("patch", "epoch"), "tile", None), P("patch")),
        check_vma=False,
    )
```

```python
import functools
import math

import jax
import jax.numpy as jnp
from jax import lax
from jax.experimental import pallas as pl
from jax.experimental.pallas import tpu as pltpu
from jax.sharding import PartitionSpec as P

STAMP = 32
HALF = 7
SIGMAS = (1.0, 2.0, 3.5)
PSF = 1.5
RH = 16
DH = 8
PAD = 64
F32 = jnp.float32
BF16 = jnp.bfloat16
HIGHEST = lax.Precision.HIGHEST
MESH = pl.DeviceIdType.MESH
CHUNKS = 4


def norm_of(sigma):
    return sum(math.exp(-o * o / (2.0 * sigma * sigma)) for o in range(-HALF, HALF + 1))


def gauss_of(offset, sigma, where=None):
    keep = jnp.abs(offset) <= HALF
    if where is not None:
        keep = keep & where
    value = jnp.exp(offset * offset * (-1.0 / (2.0 * sigma * sigma))) * (1.0 / norm_of(sigma))
    return jnp.where(keep, value, 0.0)


def band_offset(rows, cols, axis, shift):
    r = lax.broadcasted_iota(jnp.int32, (rows, cols), 0)
    c = lax.broadcasted_iota(jnp.int32, (rows, cols), 1)
    delta = (c - r) if axis == 1 else (r - c)
    return (delta - shift).astype(F32)


def split(x):
    hi = x.astype(BF16)
    return hi, (x - hi.astype(F32)).astype(BF16)


def mm(a, b):
    return jnp.dot(a, b, preferred_element_type=F32)


def mm3(a, b):
    return mm(a[0], b[0]) + mm(a[1], b[0]) + mm(a[0], b[1])


def inner_edges(tiles):
    tile = lax.axis_index("tile")
    above = jnp.where(tile > 0, 1.0, 0.0).astype(F32)
    below = jnp.where(tile < tiles - 1, 1.0, 0.0).astype(F32)
    return above, below


def fill_padded(tiles, blocks_ref, edges_ref, tpad):
    count, rows, width = blocks_ref.shape
    total = count * width
    above, below = inner_edges(tiles)
    tpad[:, :PAD] = jnp.zeros((tpad.shape[0], PAD), F32)
    tpad[:, PAD + total :] = jnp.zeros((tpad.shape[0], tpad.shape[1] - PAD - total), F32)
    for e in range(count):
        at = slice(PAD + e * width, PAD + (e + 1) * width)
        tpad[RH : RH + rows, at] = blocks_ref[e]
        tpad[:RH, at] = edges_ref[e] * above
        tpad[RH + rows :, at] = edges_ref[e] * below


def stamp_kernel(tiles, top_ref, left_ref, blocks_ref, edges_ref, sci_ref, flag_ref, out_ref, tpad, tst, sst, gst, acc):
    stamps = top_ref.shape[1]
    cols = sci_ref.shape[1]
    fill_padded(tiles, blocks_ref, edges_ref, tpad)
    lane = lax.broadcasted_iota(jnp.int32, (1, 128), 1)
    for s in range(stamps):
        top = top_ref[0, s]
        left = left_ref[0, s]
        start = left + (PAD - HALF)
        base = jnp.minimum(start // 128 * 128, tpad.shape[1] - 256)
        level = top // 8 * 8
        win = tpad[pl.ds(pl.multiple_of(level + DH, 8), 56), pl.ds(pl.multiple_of(base, 128), 256)]
        slot = 64 * (s % 2)
        moved = pltpu.roll(win, lax.rem(slot - (start - base) + 512, 256), 1)[:, :128]
        moved = pltpu.roll(moved, lax.rem(level - top + 56, 56), 0)[:48]
        at = pl.ds(128 * (s // 2), 128)
        if s % 2 == 0:
            tst[:, at] = moved
        else:
            tst[:, at] = jnp.where(lane >= 64, moved, tst[:, at])
        base = jnp.minimum(left // 128 * 128, cols - 256)
        slot = 32 * (s % 4)
        shift = lax.rem(slot - (left - base) + 512, 256)
        level = jnp.minimum(level, sci_ref.shape[0] - 40)
        back = lax.rem(level - top + 40, 40)
        where = (pl.ds(pl.multiple_of(level, 8), 40), pl.ds(pl.multiple_of(base, 128), 256))
        sci = pltpu.roll(sci_ref[where], shift, 1)[:, :128]
        sci = pltpu.roll(sci, back, 0)[:STAMP]
        good = jnp.where(flag_ref[where] == 0, 1.0, 0.0).astype(F32)
        good = pltpu.roll(good, shift, 1)[:, :128]
        good = pltpu.roll(good, back, 0)[:STAMP]
        at = pl.ds(STAMP * (s // 4), STAMP)
        if s % 4 == 0:
            sst[at, :] = sci
            gst[at, :] = good
        else:
            sst[at, :] = jnp.where(lane >= slot, sci, sst[at, :])
            gst[at, :] = jnp.where(lane >= slot, good, gst[at, :])
    offset = band_offset(STAMP, 48, 1, DH)
    parts = []
    for sigma in SIGMAS:
        g = gauss_of(offset, sigma)
        parts += [g, g * (offset * (1.0 / HALF))]
    rows = mm3(split(jnp.concatenate(parts, axis=0)), split(tst[...]))
    quads = stamps // 4
    r = lax.broadcasted_iota(jnp.int32, (256, 128), 0)
    c = lax.broadcasted_iota(jnp.int32, (256, 128), 1)
    same = (r // 64) == (c // STAMP)
    offset = ((r % 64) - (c % STAMP) - HALF).astype(F32)
    images = [None] * 12
    for k, sigma in enumerate(SIGMAS):
        lhs = split(
            jnp.concatenate(
                [rows[64 * k : 64 * k + 64, 256 * q : 256 * q + 256] for q in range(quads)], axis=0
            )
        )
        g = gauss_of(offset, sigma, same)
        for j in range(2):
            out = mm3(lhs, split(g * (offset * (1.0 / HALF)) if j else g))
            for i in range(2):
                images[4 * k + i + 2 * j] = jnp.concatenate(
                    [out[64 * q + 32 * i : 64 * q + 32 * i + 32] for q in range(quads)], axis=0
                )
    acc[...] = jnp.zeros_like(acc)
    good = gst[...]
    sci = sst[...]
    for k in range(12):
        weighted = images[k] * good
        acc[16 * k + 12 : 16 * k + 13, :] = jnp.sum(weighted * sci, axis=0, keepdims=True)
        for l in range(k + 1):
            value = jnp.sum(weighted * images[l], axis=0, keepdims=True)
            acc[16 * k + l : 16 * k + l + 1, :] = value
            if l < k:
                acc[16 * l + k : 16 * l + k + 1, :] = value
    n = acc.shape[0]
    summed = jnp.dot(acc[...], jnp.ones((128, 128), F32), precision=HIGHEST)
    r = lax.broadcasted_iota(jnp.int32, (n, 128), 0)
    c = lax.broadcasted_iota(jnp.int32, (n, 128), 1)
    summed = jnp.where(r % 16 == c, summed, 0.0)
    r = lax.broadcasted_iota(jnp.int32, (16, n), 0)
    c = lax.broadcasted_iota(jnp.int32, (16, n), 1)
    pick = jnp.where(c // 16 == r, 1.0, 0.0).astype(F32)
    out_ref[...] = jnp.dot(pick, summed, precision=HIGHEST)


def solve_system(system):
    r = lax.broadcasted_iota(jnp.int32, (16, 128), 0)
    c = lax.broadcasted_iota(jnp.int32, (16, 128), 1)
    diag = (r == c) & (r < 12)
    trace = jnp.sum(jnp.where(diag, system, 0.0), keepdims=True)
    m = system + jnp.where(diag, 0.05 * trace / 12.0, 0.0)
    for p in range(12):
        row = m[p : p + 1, :] / m[p : p + 1, p : p + 1]
        m = jnp.where(r == p, row, m - m[:, p : p + 1] * row)
    return m


def row_sizes(rows):
    half = (rows + 2 * DH) // 2 // 16 * 16
    return half, rows + 2 * DH - half


def row_bands(rows, ahi, alo):
    rest = row_sizes(rows)[1]
    offset = band_offset(rest, rest + 2 * DH, 1, DH)
    for k, sigma in enumerate(SIGMAS):
        g = gauss_of(offset, sigma)
        for i in range(2):
            ahi[2 * k + i], alo[2 * k + i] = split(g * (offset * (1.0 / HALF)) if i else g)


def row_stage(b, rows, tpad, phi, plo, ahi, alo):
    half, rest = row_sizes(rows)
    src = split(tpad[b * half : b * half + rest + 2 * DH, :])
    keep = half if b == 0 else rest

    def one(s, _):
        hi, lo = split(mm3((ahi[s], alo[s]), src))
        phi[s, b * half : b * half + keep, :] = hi[:keep]
        plo[s, b * half : b * half + keep, :] = lo[:keep]
        return _

    lax.fori_loop(0, 6, one, 0)


def apply_fit(tiles, system, halo_ref, sci_ref, det_ref, coef_ref, phi, plo, dpad):
    rows, cols = sci_ref.shape
    drows = rows + 2 * DH
    solved = solve_system(system)
    r = lax.broadcasted_iota(jnp.int32, (16, 128), 0)
    c = lax.broadcasted_iota(jnp.int32, (16, 128), 1)
    coef = jnp.sum(jnp.where(r == c, solved[:, 12:13], 0.0), axis=0, keepdims=True)
    coef_ref[...] = coef[:, :12]
    offset = band_offset(256 + 2 * PAD, 256, 0, PAD)
    scaled = offset * (1.0 / HALF)
    mats = []
    for k, sigma in enumerate(SIGMAS):
        g = gauss_of(offset, sigma)
        for i in range(2):
            a = solved[4 * k + i : 4 * k + i + 1, 12:13]
            b = solved[4 * k + i + 2 : 4 * k + i + 3, 12:13]
            mats.append(split(g * (a + b * scaled)))
    dpad[:, :PAD] = jnp.zeros((drows, PAD), F32)
    dpad[:, PAD + cols :] = jnp.zeros((drows, PAD), F32)
    above, below = inner_edges(tiles)
    for j in range(cols // 256):
        at = slice(256 * j, 256 * j + 256 + 2 * PAD)
        model = jnp.zeros((drows, 256), F32)
        for s in range(6):
            model = model + mm3((phi[s, :, at], plo[s, :, at]), mats[s])
        here = slice(256 * j, 256 * j + 256)
        to = slice(PAD + 256 * j, PAD + 256 * j + 256)
        dpad[:DH, to] = (halo_ref[:, here] - model[:DH]) * above
        dpad[DH : DH + rows, to] = sci_ref[:, here] - model[DH : DH + rows]
        dpad[DH + rows :, to] = (halo_ref[:, here] - model[DH + rows :]) * below
    psf_row = split(gauss_of(band_offset(128, 128 + 2 * DH, 1, DH), PSF))
    psf_col = split(gauss_of(offset, PSF))
    for b in range(rows // 128):
        inner = mm3(psf_row, split(dpad[128 * b : 128 * b + 128 + 2 * DH, :]))
        hi, lo = split(inner)
        for j in range(cols // 256):
            at = slice(256 * j, 256 * j + 256 + 2 * PAD)
            det_ref[128 * b : 128 * b + 128, 256 * j : 256 * j + 256] = mm3(
                (hi[:, at], lo[:, at]), psf_col
            )


def ring_place(count, paired):
    if not paired:
        return lambda e: e, lambda p: p
    half = count // 2

    def position(e):
        z, y = e // 2, e % 2
        return z + y * (count - 1 - 2 * z)

    def index(p):
        far = p // half
        return 2 * p * (1 - far) + far * (2 * (count - 1 - p) + 1)

    return position, index


def gather_kernel(count, paired, own_ref, sci_ref, blocks, edges, halo, ssem, rsem, esend, erecv, hsem, lsem):
    me = lax.axis_index("epoch")
    tile = lax.axis_index("tile")
    position, index = ring_place(count, paired)
    pos = position(me)
    ring = (index(lax.rem(pos + 1, count)), index(lax.rem(pos + count - 1, count)))
    other = 1 - tile
    barrier = pltpu.get_barrier_semaphore()
    for e in ring:
        pl.semaphore_signal(barrier, inc=1, device_id={"epoch": e}, device_id_type=MESH)
    pl.semaphore_signal(barrier, inc=1, device_id={"tile": other}, device_id_type=MESH)
    keep = pltpu.make_async_copy(own_ref, blocks.at[me], lsem)
    keep.start()
    pl.semaphore_wait(barrier, 3)
    rows = own_ref.shape[0]
    chunk = rows // CHUNKS

    def move(way, step, c, origin, src=None):
        at = pl.ds(c * chunk, chunk)
        return pltpu.make_async_remote_copy(
            src_ref=blocks.at[origin, at] if src is None else src.at[at],
            dst_ref=blocks.at[origin, at],
            send_sem=ssem.at[way, step, c],
            recv_sem=rsem.at[way, step, c],
            device_id={"epoch": ring[way]},
            device_id_type=MESH,
        )

    def edge(step, origin, src=None):
        at = pl.ds(pl.multiple_of(other * (rows - RH), 8), RH)
        return pltpu.make_async_remote_copy(
            src_ref=blocks.at[origin, at] if src is None else src.at[at],
            dst_ref=edges.at[origin],
            send_sem=esend.at[step],
            recv_sem=erecv.at[step],
            device_id={"tile": other},
            device_id_type=MESH,
        )

    reach = count // 2

    def has(way, step, c):
        return step < reach or count % 2 == 1 or (c < CHUNKS // 2) == (way == 0)

    started = []
    for c in range(CHUNKS):
        for way in range(2):
            if has(way, 1, c):
                started.append(move(way, 0, c, me, own_ref))
                started[-1].start()
    first = edge(0, me, own_ref)
    first.start()
    at = pl.ds(pl.multiple_of(other * (sci_ref.shape[0] - DH), 8), DH)
    science = pltpu.make_async_remote_copy(
        src_ref=sci_ref.at[at],
        dst_ref=halo,
        send_sem=hsem.at[0],
        recv_sem=hsem.at[1],
        device_id={"tile": other},
        device_id_type=MESH,
    )
    science.start()
    side = [first]
    for step in range(1, reach + 1):
        origins = [index(lax.rem(pos + (count - step if way == 0 else step), count)) for way in range(2)]
        halves = step == reach and count % 2 == 0
        for c in range(CHUNKS):
            for way in range(2):
                d = c if way == 0 or not halves else (c + CHUNKS // 2) % CHUNKS
                if not has(way, step, d):
                    continue
                move(way, step - 1, d, origins[way]).wait_recv()
                if step < reach and has(way, step + 1, d):
                    started.append(move(way, step, d, origins[way]))
                    started[-1].start()
        for origin in origins[:1] if halves else origins:
            side.append(edge(len(side), origin))
            side[-1].start()
    for copy in started:
        copy.wait_send()
    for copy in side:
        copy.wait()
    science.wait()
    keep.wait()


def fit_kernel(
    epochs, tiles, part, blocks_ref, edges_ref, halo_ref, sci_ref, det_ref, coef_ref,
    tpad, slots, phi, plo, dpad, ahi, alo, ssem, rsem, lsem,
):
    count = epochs * tiles
    me = lax.axis_index("epoch") * tiles + lax.axis_index("tile")
    barrier = pltpu.get_barrier_semaphore()

    def where(d):
        peer = lax.rem(me + d, count)
        return {"epoch": peer // tiles, "tile": peer % tiles}

    def greet(d, _):
        pl.semaphore_signal(barrier, inc=1, device_id=where(d), device_id_type=MESH)
        return _

    lax.fori_loop(1, count, greet, 0)
    fill_padded(tiles, blocks_ref, edges_ref, tpad)
    row_bands(sci_ref.shape[0], ahi, alo)
    row_stage(0, sci_ref.shape[0], tpad, phi, plo, ahi, alo)
    keep = pltpu.make_async_copy(part, slots.at[me], lsem)
    keep.start()
    pl.semaphore_wait(barrier, count - 1)

    def copy(d, slot):
        return pltpu.make_async_remote_copy(
            src_ref=part,
            dst_ref=slots.at[slot],
            send_sem=ssem.at[d],
            recv_sem=rsem.at[d],
            device_id=where(d),
            device_id_type=MESH,
        )

    def send(d, _):
        copy(d, me).start()
        return _

    lax.fori_loop(1, count, send, 0)
    row_stage(1, sci_ref.shape[0], tpad, phi, plo, ahi, alo)
    keep.wait()

    def finish(d, _):
        made = copy(d, lax.rem(me + count - d, count))
        made.wait_send()
        made.wait_recv()
        return _

    lax.fori_loop(1, count, finish, 0)
    system = jnp.sum(slots[...], axis=0)
    apply_fit(tiles, system, halo_ref, sci_ref, det_ref, coef_ref, phi, plo, dpad)


def vmem_specs(count):
    return [pl.BlockSpec(memory_space=pltpu.VMEM)] * count


def local(epochs, tiles, paired, template, science, flags, stamp_rows, stamp_cols):
    sci = science[0]
    rows, cols = sci.shape
    width = template.shape[1]
    ext_rows = rows + 2 * RH
    padded = cols + 2 * PAD
    stamps = stamp_rows.shape[1]
    reach = epochs // 2
    blocks, edges, halo = pl.pallas_call(
        functools.partial(gather_kernel, epochs, paired),
        out_shape=(
            jax.ShapeDtypeStruct((epochs, rows, width), F32),
            jax.ShapeDtypeStruct((epochs, RH, width), F32),
            jax.ShapeDtypeStruct((DH, cols), F32),
        ),
        in_specs=[pl.BlockSpec(memory_space=pl.ANY)] * 2,
        out_specs=tuple(vmem_specs(3)),
        scratch_shapes=[
            pltpu.SemaphoreType.DMA((2, reach, CHUNKS)),
            pltpu.SemaphoreType.DMA((2, reach, CHUNKS)),
            pltpu.SemaphoreType.DMA((epochs,)),
            pltpu.SemaphoreType.DMA((epochs,)),
            pltpu.SemaphoreType.DMA((2,)),
            pltpu.SemaphoreType.DMA,
        ],
        compiler_params=pltpu.CompilerParams(collective_id=0, has_side_effects=True),
        name="gather",
    )(template, sci)
    partial = pl.pallas_call(
        functools.partial(stamp_kernel, tiles),
        out_shape=jax.ShapeDtypeStruct((16, 128), F32),
        in_specs=[pl.BlockSpec(memory_space=pltpu.SMEM)] * 2 + vmem_specs(4),
        out_specs=pl.BlockSpec(memory_space=pltpu.VMEM),
        scratch_shapes=[
            pltpu.VMEM((ext_rows, padded), F32),
            pltpu.VMEM((48, 64 * stamps), F32),
            pltpu.VMEM((STAMP * stamps // 4, 128), F32),
            pltpu.VMEM((STAMP * stamps // 4, 128), F32),
            pltpu.VMEM((192, 128), F32),
        ],
        name="stamps",
    )(stamp_rows, stamp_cols, blocks, edges, sci, flags[0])
    drows = rows + 2 * DH
    rest = drows - drows // 2 // 16 * 16
    detection, coefficients = pl.pallas_call(
        functools.partial(fit_kernel, epochs, tiles),
        out_shape=(
            jax.ShapeDtypeStruct((rows, cols), F32),
            jax.ShapeDtypeStruct((1, 12), F32),
        ),
        in_specs=vmem_specs(5),
        out_specs=tuple(vmem_specs(2)),
        scratch_shapes=[
            pltpu.VMEM((ext_rows, padded), F32),
            pltpu.VMEM((epochs * tiles, 16, 128), F32),
            pltpu.VMEM((6, drows, padded), BF16),
            pltpu.VMEM((6, drows, padded), BF16),
            pltpu.VMEM((drows, padded), F32),
            pltpu.VMEM((6, rest, rest + 2 * DH), BF16),
            pltpu.VMEM((6, rest, rest + 2 * DH), BF16),
            pltpu.SemaphoreType.DMA((epochs * tiles,)),
            pltpu.SemaphoreType.DMA((epochs * tiles,)),
            pltpu.SemaphoreType.DMA,
        ],
        compiler_params=pltpu.CompilerParams(
            collective_id=1, has_side_effects=True, vmem_limit_bytes=48 * 1024 * 1024
        ),
        name="fit",
    )(partial, blocks, edges, halo, sci)
    return (detection[None], coefficients.reshape(12))


def solution(mesh):
    line = mesh.devices[0, :, 0]
    columns = {tuple(getattr(d, "coords", (0, 0)))[:2] for d in line}
    paired = len(columns) == 2 and len(line) % 2 == 0
    return jax.shard_map(
        functools.partial(local, mesh.shape["epoch"], mesh.shape["tile"], paired),
        mesh=mesh,
        in_specs=(
            P(("patch", "tile"), "epoch"),
            P(("patch", "epoch"), "tile", None),
            P(("patch", "epoch"), "tile", None),
            P(("patch", "epoch"), "tile"),
            P(("patch", "epoch"), "tile"),
        ),
        out_specs=(P(("patch", "epoch"), "tile", None), P("patch")),
        check_vma=False,
    )
```

```python
import functools
import math

import jax
import jax.numpy as jnp
from jax import lax
from jax.experimental import pallas as pl
from jax.experimental.pallas import tpu as pltpu
from jax.sharding import PartitionSpec as P

STAMP = 32
HALF = 7
SIGMAS = (1.0, 2.0, 3.5)
PSF = 1.5
RH = 16
DH = 8
PAD = 64
F32 = jnp.float32
BF16 = jnp.bfloat16
HIGHEST = lax.Precision.HIGHEST
MESH = pl.DeviceIdType.MESH
BLOCK = 64
CHUNKS = 4


def norm_of(sigma):
    return sum(math.exp(-o * o / (2.0 * sigma * sigma)) for o in range(-HALF, HALF + 1))


def gauss_of(offset, sigma, where=None):
    keep = jnp.abs(offset) <= HALF
    if where is not None:
        keep = keep & where
    value = jnp.exp(offset * offset * (-1.0 / (2.0 * sigma * sigma))) * (1.0 / norm_of(sigma))
    return jnp.where(keep, value, 0.0)


def band_offset(rows, cols, axis, shift):
    r = lax.broadcasted_iota(jnp.int32, (rows, cols), 0)
    c = lax.broadcasted_iota(jnp.int32, (rows, cols), 1)
    delta = (c - r) if axis == 1 else (r - c)
    return (delta - shift).astype(F32)


def split(x):
    hi = x.astype(BF16)
    return hi, (x - hi.astype(F32)).astype(BF16)


def mm(a, b):
    return jnp.dot(a, b, preferred_element_type=F32)


def mm3(a, b):
    return mm(a[0], b[0]) + mm(a[1], b[0]) + mm(a[0], b[1])


def inner_edges(tiles):
    tile = lax.axis_index("tile")
    above = jnp.where(tile > 0, 1.0, 0.0).astype(F32)
    below = jnp.where(tile < tiles - 1, 1.0, 0.0).astype(F32)
    return above, below


def fill_padded(tiles, blocks_ref, edges_ref, tpad):
    count, rows, width = blocks_ref.shape
    total = count * width
    above, below = inner_edges(tiles)
    tpad[:, :PAD] = jnp.zeros((tpad.shape[0], PAD), F32)
    tpad[:, PAD + total :] = jnp.zeros((tpad.shape[0], tpad.shape[1] - PAD - total), F32)
    for e in range(count):
        at = slice(PAD + e * width, PAD + (e + 1) * width)
        tpad[RH : RH + rows, at] = blocks_ref[e]
        tpad[:RH, at] = edges_ref[e] * above
        tpad[RH + rows :, at] = edges_ref[e] * below


def stamp_kernel(tiles, top_ref, left_ref, blocks_ref, edges_ref, sci_ref, flag_ref, out_ref, tpad, tst, sst, gst, acc):
    stamps = top_ref.shape[1]
    cols = sci_ref.shape[1]
    fill_padded(tiles, blocks_ref, edges_ref, tpad)
    lane = lax.broadcasted_iota(jnp.int32, (1, 128), 1)
    for s in range(stamps):
        top = top_ref[0, s]
        left = left_ref[0, s]
        start = left + (PAD - HALF)
        base = jnp.minimum(start // 128 * 128, tpad.shape[1] - 256)
        level = top // 8 * 8
        win = tpad[pl.ds(pl.multiple_of(level + DH, 8), 56), pl.ds(pl.multiple_of(base, 128), 256)]
        slot = 64 * (s % 2)
        moved = pltpu.roll(win, lax.rem(slot - (start - base) + 512, 256), 1)[:, :128]
        moved = pltpu.roll(moved, lax.rem(level - top + 56, 56), 0)[:48]
        at = pl.ds(128 * (s // 2), 128)
        if s % 2 == 0:
            tst[:, at] = moved
        else:
            tst[:, at] = jnp.where(lane >= 64, moved, tst[:, at])
        base = jnp.minimum(left // 128 * 128, cols - 256)
        slot = 32 * (s % 4)
        shift = lax.rem(slot - (left - base) + 512, 256)
        level = jnp.minimum(level, sci_ref.shape[0] - 40)
        back = lax.rem(level - top + 40, 40)
        where = (pl.ds(pl.multiple_of(level, 8), 40), pl.ds(pl.multiple_of(base, 128), 256))
        sci = pltpu.roll(sci_ref[where], shift, 1)[:, :128]
        sci = pltpu.roll(sci, back, 0)[:STAMP]
        good = jnp.where(flag_ref[where] == 0, 1.0, 0.0).astype(F32)
        good = pltpu.roll(good, shift, 1)[:, :128]
        good = pltpu.roll(good, back, 0)[:STAMP]
        at = pl.ds(STAMP * (s // 4), STAMP)
        if s % 4 == 0:
            sst[at, :] = sci
            gst[at, :] = good
        else:
            sst[at, :] = jnp.where(lane >= slot, sci, sst[at, :])
            gst[at, :] = jnp.where(lane >= slot, good, gst[at, :])
    offset = band_offset(STAMP, 48, 1, DH)
    parts = []
    for sigma in SIGMAS:
        g = gauss_of(offset, sigma)
        parts += [g, g * (offset * (1.0 / HALF))]
    rows = mm3(split(jnp.concatenate(parts, axis=0)), split(tst[...]))
    quads = stamps // 4
    r = lax.broadcasted_iota(jnp.int32, (256, 128), 0)
    c = lax.broadcasted_iota(jnp.int32, (256, 128), 1)
    same = (r // 64) == (c // STAMP)
    offset = ((r % 64) - (c % STAMP) - HALF).astype(F32)
    images = [None] * 12
    for k, sigma in enumerate(SIGMAS):
        lhs = split(
            jnp.concatenate(
                [rows[64 * k : 64 * k + 64, 256 * q : 256 * q + 256] for q in range(quads)], axis=0
            )
        )
        g = gauss_of(offset, sigma, same)
        for j in range(2):
            out = mm3(lhs, split(g * (offset * (1.0 / HALF)) if j else g))
            for i in range(2):
                images[4 * k + i + 2 * j] = jnp.concatenate(
                    [out[64 * q + 32 * i : 64 * q + 32 * i + 32] for q in range(quads)], axis=0
                )
    acc[...] = jnp.zeros_like(acc)
    good = gst[...]
    sci = sst[...]
    for k in range(12):
        weighted = images[k] * good
        acc[16 * k + 12 : 16 * k + 13, :] = jnp.sum(weighted * sci, axis=0, keepdims=True)
        for l in range(k + 1):
            value = jnp.sum(weighted * images[l], axis=0, keepdims=True)
            acc[16 * k + l : 16 * k + l + 1, :] = value
            if l < k:
                acc[16 * l + k : 16 * l + k + 1, :] = value
    n = acc.shape[0]
    summed = jnp.dot(acc[...], jnp.ones((128, 128), F32), precision=HIGHEST)
    r = lax.broadcasted_iota(jnp.int32, (n, 128), 0)
    c = lax.broadcasted_iota(jnp.int32, (n, 128), 1)
    summed = jnp.where(r % 16 == c, summed, 0.0)
    r = lax.broadcasted_iota(jnp.int32, (16, n), 0)
    c = lax.broadcasted_iota(jnp.int32, (16, n), 1)
    pick = jnp.where(c // 16 == r, 1.0, 0.0).astype(F32)
    out_ref[...] = jnp.dot(pick, summed, precision=HIGHEST)


def solve_system(system):
    r = lax.broadcasted_iota(jnp.int32, (16, 128), 0)
    c = lax.broadcasted_iota(jnp.int32, (16, 128), 1)
    diag = (r == c) & (r < 12)
    trace = jnp.sum(jnp.where(diag, system, 0.0), keepdims=True)
    m = system + jnp.where(diag, 0.05 * trace / 12.0, 0.0)
    for p in range(12):
        row = m[p : p + 1, :] / m[p : p + 1, p : p + 1]
        m = jnp.where(r == p, row, m - m[:, p : p + 1] * row)
    return m


def stacked_band(g):
    hi, lo = split(g)
    return jnp.concatenate([hi, lo, hi], axis=1)


def stacked_rows(x):
    hi, lo = split(x)
    return jnp.concatenate([hi, hi, lo], axis=0)


def block_starts(count):
    starts = list(range(0, count - BLOCK + 1, BLOCK))
    return starts if count % BLOCK == 0 else starts + [count - BLOCK]


def row_bands(bands):
    offset = band_offset(BLOCK, BLOCK + 2 * DH, 1, DH)
    for k, sigma in enumerate(SIGMAS):
        g = gauss_of(offset, sigma)
        for i in range(2):
            at = slice(BLOCK * (2 * k + i), BLOCK * (2 * k + i + 1))
            bands[at, :] = stacked_band(g * (offset * (1.0 / HALF)) if i else g)


def row_stage(start, tpad, phi, plo, bands):
    out = mm(bands[...], stacked_rows(tpad[start : start + BLOCK + 2 * DH, :]))
    for s in range(6):
        hi, lo = split(out[BLOCK * s : BLOCK * (s + 1)])
        phi[s, start : start + BLOCK, :] = hi
        plo[s, start : start + BLOCK, :] = lo


def apply_fit(tiles, system, halo_ref, sci_ref, det_ref, coef_ref, phi, plo, dpad):
    rows, cols = sci_ref.shape
    drows = rows + 2 * DH
    solved = solve_system(system)
    r = lax.broadcasted_iota(jnp.int32, (16, 128), 0)
    c = lax.broadcasted_iota(jnp.int32, (16, 128), 1)
    coef = jnp.sum(jnp.where(r == c, solved[:, 12:13], 0.0), axis=0, keepdims=True)
    coef_ref[...] = coef[:, :12]
    offset = band_offset(256 + 2 * PAD, 256, 0, PAD)
    scaled = offset * (1.0 / HALF)
    mats = []
    for k, sigma in enumerate(SIGMAS):
        g = gauss_of(offset, sigma)
        for i in range(2):
            a = solved[4 * k + i : 4 * k + i + 1, 12:13]
            b = solved[4 * k + i + 2 : 4 * k + i + 3, 12:13]
            mats.append(split(g * (a + b * scaled)))
    dpad[:, :PAD] = jnp.zeros((drows, PAD), F32)
    dpad[:, PAD + cols :] = jnp.zeros((drows, PAD), F32)
    above, below = inner_edges(tiles)
    for j in range(cols // 256):
        at = slice(256 * j, 256 * j + 256 + 2 * PAD)
        model = jnp.zeros((drows, 256), F32)
        for s in range(6):
            model = model + mm3((phi[s, :, at], plo[s, :, at]), mats[s])
        here = slice(256 * j, 256 * j + 256)
        to = slice(PAD + 256 * j, PAD + 256 * j + 256)
        dpad[:DH, to] = (halo_ref[:, here] - model[:DH]) * above
        dpad[DH : DH + rows, to] = sci_ref[:, here] - model[DH : DH + rows]
        dpad[DH + rows :, to] = (halo_ref[:, here] - model[DH + rows :]) * below
    psf_row = stacked_band(gauss_of(band_offset(BLOCK, BLOCK + 2 * DH, 1, DH), PSF))
    psf_col = split(gauss_of(offset, PSF))
    inner = [
        mm(psf_row, stacked_rows(dpad[start : start + BLOCK + 2 * DH, :]))
        for start in range(0, rows, BLOCK)
    ]
    for b in range(rows // 128):
        hi, lo = split(jnp.concatenate(inner[2 * b : 2 * b + 2], axis=0))
        for j in range(cols // 256):
            at = slice(256 * j, 256 * j + 256 + 2 * PAD)
            det_ref[128 * b : 128 * b + 128, 256 * j : 256 * j + 256] = mm3(
                (hi[:, at], lo[:, at]), psf_col
            )


def ring_place(count, paired):
    if not paired:
        return lambda e: e, lambda p: p
    half = count // 2

    def position(e):
        z, y = e // 2, e % 2
        return z + y * (count - 1 - 2 * z)

    def index(p):
        far = p // half
        return 2 * p * (1 - far) + far * (2 * (count - 1 - p) + 1)

    return position, index


def gather_kernel(count, paired, own_ref, sci_ref, blocks, edges, halo, ssem, rsem, esend, erecv, hsem, lsem):
    me = lax.axis_index("epoch")
    tile = lax.axis_index("tile")
    position, index = ring_place(count, paired)
    pos = position(me)
    ring = (index(lax.rem(pos + 1, count)), index(lax.rem(pos + count - 1, count)))
    other = 1 - tile
    barrier = pltpu.get_barrier_semaphore()
    for e in ring:
        pl.semaphore_signal(barrier, inc=1, device_id={"epoch": e}, device_id_type=MESH)
    pl.semaphore_signal(barrier, inc=1, device_id={"tile": other}, device_id_type=MESH)
    keep = pltpu.make_async_copy(own_ref, blocks.at[me], lsem)
    keep.start()
    pl.semaphore_wait(barrier, 3)
    rows = own_ref.shape[0]
    chunk = rows // CHUNKS

    def move(way, step, c, origin, src=None):
        at = pl.ds(c * chunk, chunk)
        return pltpu.make_async_remote_copy(
            src_ref=blocks.at[origin, at] if src is None else src.at[at],
            dst_ref=blocks.at[origin, at],
            send_sem=ssem.at[way, step, c],
            recv_sem=rsem.at[way, step, c],
            device_id={"epoch": ring[way]},
            device_id_type=MESH,
        )

    def edge(step, origin, src=None):
        at = pl.ds(pl.multiple_of(other * (rows - RH), 8), RH)
        return pltpu.make_async_remote_copy(
            src_ref=blocks.at[origin, at] if src is None else src.at[at],
            dst_ref=edges.at[origin],
            send_sem=esend.at[step],
            recv_sem=erecv.at[step],
            device_id={"tile": other},
            device_id_type=MESH,
        )

    reach = count // 2

    def has(way, step, c):
        return step < reach or count % 2 == 1 or (c < CHUNKS // 2) == (way == 0)

    started = []
    for c in range(CHUNKS):
        for way in range(2):
            if has(way, 1, c):
                started.append(move(way, 0, c, me, own_ref))
                started[-1].start()
    first = edge(0, me, own_ref)
    first.start()
    at = pl.ds(pl.multiple_of(other * (sci_ref.shape[0] - DH), 8), DH)
    science = pltpu.make_async_remote_copy(
        src_ref=sci_ref.at[at],
        dst_ref=halo,
        send_sem=hsem.at[0],
        recv_sem=hsem.at[1],
        device_id={"tile": other},
        device_id_type=MESH,
    )
    science.start()
    side = [first]
    for step in range(1, reach + 1):
        origins = [index(lax.rem(pos + (count - step if way == 0 else step), count)) for way in range(2)]
        halves = step == reach and count % 2 == 0
        for c in range(CHUNKS):
            for way in range(2):
                d = c if way == 0 or not halves else (c + CHUNKS // 2) % CHUNKS
                if not has(way, step, d):
                    continue
                move(way, step - 1, d, origins[way]).wait_recv()
                if step < reach and has(way, step + 1, d):
                    started.append(move(way, step, d, origins[way]))
                    started[-1].start()
        for origin in origins[:1] if halves else origins:
            side.append(edge(len(side), origin))
            side[-1].start()
    for copy in started:
        copy.wait_send()
    for copy in side:
        copy.wait()
    science.wait()
    keep.wait()


def fit_kernel(
    epochs, tiles, part, blocks_ref, edges_ref, halo_ref, sci_hbm, det_ref, coef_ref,
    tpad, sci_in, slots, phi, plo, dpad, bands, ssem, rsem, lsem, isem,
):
    count = epochs * tiles
    me = lax.axis_index("epoch") * tiles + lax.axis_index("tile")
    barrier = pltpu.get_barrier_semaphore()

    def where(d):
        peer = lax.rem(me + d, count)
        return {"epoch": peer // tiles, "tile": peer % tiles}

    def greet(d, _):
        pl.semaphore_signal(barrier, inc=1, device_id=where(d), device_id_type=MESH)
        return _

    lax.fori_loop(1, count, greet, 0)
    fill_padded(tiles, blocks_ref, edges_ref, tpad)
    fetch = pltpu.make_async_copy(sci_hbm, sci_in, isem)
    fetch.start()
    row_bands(bands)
    starts = block_starts(dpad.shape[0])
    for start in starts[:2]:
        row_stage(start, tpad, phi, plo, bands)
    keep = pltpu.make_async_copy(part, slots.at[me], lsem)
    keep.start()
    pl.semaphore_wait(barrier, count - 1)

    def copy(d, slot):
        return pltpu.make_async_remote_copy(
            src_ref=part,
            dst_ref=slots.at[slot],
            send_sem=ssem.at[d],
            recv_sem=rsem.at[d],
            device_id=where(d),
            device_id_type=MESH,
        )

    def send(d, _):
        copy(d, me).start()
        return _

    lax.fori_loop(1, count, send, 0)
    for start in starts[2:]:
        row_stage(start, tpad, phi, plo, bands)
    keep.wait()
    fetch.wait()

    def finish(d, _):
        made = copy(d, lax.rem(me + count - d, count))
        made.wait_send()
        made.wait_recv()
        return _

    lax.fori_loop(1, count, finish, 0)
    system = jnp.sum(slots[...], axis=0)
    apply_fit(tiles, system, halo_ref, sci_in, det_ref, coef_ref, phi, plo, dpad)


def vmem_specs(count):
    return [pl.BlockSpec(memory_space=pltpu.VMEM)] * count


def local(epochs, tiles, paired, template, science, flags, stamp_rows, stamp_cols):
    sci = science[0]
    rows, cols = sci.shape
    width = template.shape[1]
    ext_rows = rows + 2 * RH
    padded = cols + 2 * PAD
    stamps = stamp_rows.shape[1]
    reach = epochs // 2
    blocks, edges, halo = pl.pallas_call(
        functools.partial(gather_kernel, epochs, paired),
        out_shape=(
            jax.ShapeDtypeStruct((epochs, rows, width), F32),
            jax.ShapeDtypeStruct((epochs, RH, width), F32),
            jax.ShapeDtypeStruct((DH, cols), F32),
        ),
        in_specs=[pl.BlockSpec(memory_space=pl.ANY)] * 2,
        out_specs=tuple(vmem_specs(3)),
        scratch_shapes=[
            pltpu.SemaphoreType.DMA((2, reach, CHUNKS)),
            pltpu.SemaphoreType.DMA((2, reach, CHUNKS)),
            pltpu.SemaphoreType.DMA((epochs,)),
            pltpu.SemaphoreType.DMA((epochs,)),
            pltpu.SemaphoreType.DMA((2,)),
            pltpu.SemaphoreType.DMA,
        ],
        compiler_params=pltpu.CompilerParams(collective_id=0, has_side_effects=True),
        name="gather",
    )(template, sci)
    partial = pl.pallas_call(
        functools.partial(stamp_kernel, tiles),
        out_shape=jax.ShapeDtypeStruct((16, 128), F32),
        in_specs=[pl.BlockSpec(memory_space=pltpu.SMEM)] * 2 + vmem_specs(4),
        out_specs=pl.BlockSpec(memory_space=pltpu.VMEM),
        scratch_shapes=[
            pltpu.VMEM((ext_rows, padded), F32),
            pltpu.VMEM((48, 64 * stamps), F32),
            pltpu.VMEM((STAMP * stamps // 4, 128), F32),
            pltpu.VMEM((STAMP * stamps // 4, 128), F32),
            pltpu.VMEM((192, 128), F32),
        ],
        name="stamps",
    )(stamp_rows, stamp_cols, blocks, edges, sci, flags[0])
    drows = rows + 2 * DH
    detection, coefficients = pl.pallas_call(
        functools.partial(fit_kernel, epochs, tiles),
        out_shape=(
            jax.ShapeDtypeStruct((rows, cols), F32),
            jax.ShapeDtypeStruct((1, 12), F32),
        ),
        in_specs=vmem_specs(4) + [pl.BlockSpec(memory_space=pl.ANY)],
        out_specs=tuple(vmem_specs(2)),
        scratch_shapes=[
            pltpu.VMEM((ext_rows, padded), F32),
            pltpu.VMEM((rows, cols), F32),
            pltpu.VMEM((epochs * tiles, 16, 128), F32),
            pltpu.VMEM((6, drows, padded), BF16),
            pltpu.VMEM((6, drows, padded), BF16),
            pltpu.VMEM((drows, padded), F32),
            pltpu.VMEM((6 * BLOCK, 3 * (BLOCK + 2 * DH)), BF16),
            pltpu.SemaphoreType.DMA((epochs * tiles,)),
            pltpu.SemaphoreType.DMA((epochs * tiles,)),
            pltpu.SemaphoreType.DMA,
            pltpu.SemaphoreType.DMA,
        ],
        compiler_params=pltpu.CompilerParams(
            collective_id=1, has_side_effects=True, vmem_limit_bytes=48 * 1024 * 1024
        ),
        name="fit",
    )(partial, blocks, edges, halo, sci)
    return (detection[None], coefficients.reshape(12))


def solution(mesh):
    line = mesh.devices[0, :, 0]
    columns = {tuple(getattr(d, "coords", (0, 0)))[:2] for d in line}
    paired = len(columns) == 2 and len(line) % 2 == 0
    return jax.shard_map(
        functools.partial(local, mesh.shape["epoch"], mesh.shape["tile"], paired),
        mesh=mesh,
        in_specs=(
            P(("patch", "tile"), "epoch"),
            P(("patch", "epoch"), "tile", None),
            P(("patch", "epoch"), "tile", None),
            P(("patch", "epoch"), "tile"),
            P(("patch", "epoch"), "tile"),
        ),
        out_specs=(P(("patch", "epoch"), "tile", None), P("patch")),
        check_vma=False,
    )
```

```python
import functools
import math

import jax
import jax.numpy as jnp
from jax import lax
from jax.experimental import pallas as pl
from jax.experimental.pallas import tpu as pltpu
from jax.sharding import PartitionSpec as P

STAMP = 32
HALF = 7
SIGMAS = (1.0, 2.0, 3.5)
PSF = 1.5
RH = 16
DH = 8
PAD = 64
F32 = jnp.float32
BF16 = jnp.bfloat16
HIGHEST = lax.Precision.HIGHEST
MESH = pl.DeviceIdType.MESH
BLOCK = 64
CHUNKS = 4


def norm_of(sigma):
    return sum(math.exp(-o * o / (2.0 * sigma * sigma)) for o in range(-HALF, HALF + 1))


def gauss_of(offset, sigma, where=None):
    keep = jnp.abs(offset) <= HALF
    if where is not None:
        keep = keep & where
    value = jnp.exp(offset * offset * (-1.0 / (2.0 * sigma * sigma))) * (1.0 / norm_of(sigma))
    return jnp.where(keep, value, 0.0)


def band_offset(rows, cols, axis, shift):
    r = lax.broadcasted_iota(jnp.int32, (rows, cols), 0)
    c = lax.broadcasted_iota(jnp.int32, (rows, cols), 1)
    delta = (c - r) if axis == 1 else (r - c)
    return (delta - shift).astype(F32)


def split(x):
    hi = x.astype(BF16)
    return hi, (x - hi.astype(F32)).astype(BF16)


def mm(a, b):
    return jnp.dot(a, b, preferred_element_type=F32)


def mm3(a, b):
    return mm(a[0], b[0]) + mm(a[1], b[0]) + mm(a[0], b[1])


def inner_edges(tiles):
    tile = lax.axis_index("tile")
    above = jnp.where(tile > 0, 1.0, 0.0).astype(F32)
    below = jnp.where(tile < tiles - 1, 1.0, 0.0).astype(F32)
    return above, below


def fill_padded(tiles, blocks_ref, edges_ref, tpad):
    count, rows, width = blocks_ref.shape
    total = count * width
    above, below = inner_edges(tiles)
    tpad[:, :PAD] = jnp.zeros((tpad.shape[0], PAD), F32)
    tpad[:, PAD + total :] = jnp.zeros((tpad.shape[0], tpad.shape[1] - PAD - total), F32)
    for e in range(count):
        at = slice(PAD + e * width, PAD + (e + 1) * width)
        tpad[RH : RH + rows, at] = blocks_ref[e]
        tpad[:RH, at] = edges_ref[e] * above
        tpad[RH + rows :, at] = edges_ref[e] * below


def stamp_kernel(tiles, top_ref, left_ref, blocks_ref, edges_ref, sci_ref, flag_ref, out_ref, tpad, tst, sst, gst, acc):
    stamps = top_ref.shape[1]
    cols = sci_ref.shape[1]
    fill_padded(tiles, blocks_ref, edges_ref, tpad)
    lane = lax.broadcasted_iota(jnp.int32, (1, 128), 1)
    for s in range(stamps):
        top = top_ref[0, s]
        left = left_ref[0, s]
        start = left + (PAD - HALF)
        base = jnp.minimum(start // 128 * 128, tpad.shape[1] - 256)
        level = top // 8 * 8
        win = tpad[pl.ds(pl.multiple_of(level + DH, 8), 56), pl.ds(pl.multiple_of(base, 128), 256)]
        slot = 64 * (s % 2)
        moved = pltpu.roll(win, lax.rem(slot - (start - base) + 512, 256), 1)[:, :128]
        moved = pltpu.roll(moved, lax.rem(level - top + 56, 56), 0)[:48]
        at = pl.ds(128 * (s // 2), 128)
        if s % 2 == 0:
            tst[:, at] = moved
        else:
            tst[:, at] = jnp.where(lane >= 64, moved, tst[:, at])
        base = jnp.minimum(left // 128 * 128, cols - 256)
        slot = 32 * (s % 4)
        shift = lax.rem(slot - (left - base) + 512, 256)
        level = jnp.minimum(level, sci_ref.shape[0] - 40)
        back = lax.rem(level - top + 40, 40)
        where = (pl.ds(pl.multiple_of(level, 8), 40), pl.ds(pl.multiple_of(base, 128), 256))
        sci = pltpu.roll(sci_ref[where], shift, 1)[:, :128]
        sci = pltpu.roll(sci, back, 0)[:STAMP]
        good = jnp.where(flag_ref[where] == 0, 1.0, 0.0).astype(F32)
        good = pltpu.roll(good, shift, 1)[:, :128]
        good = pltpu.roll(good, back, 0)[:STAMP]
        at = pl.ds(STAMP * (s // 4), STAMP)
        if s % 4 == 0:
            sst[at, :] = sci
            gst[at, :] = good
        else:
            sst[at, :] = jnp.where(lane >= slot, sci, sst[at, :])
            gst[at, :] = jnp.where(lane >= slot, good, gst[at, :])
    offset = band_offset(STAMP, 48, 1, DH)
    parts = []
    for sigma in SIGMAS:
        g = gauss_of(offset, sigma)
        parts += [g, g * (offset * (1.0 / HALF))]
    rows = mm3(split(jnp.concatenate(parts, axis=0)), split(tst[...]))
    quads = stamps // 4
    r = lax.broadcasted_iota(jnp.int32, (256, 128), 0)
    c = lax.broadcasted_iota(jnp.int32, (256, 128), 1)
    same = (r // 64) == (c // STAMP)
    offset = ((r % 64) - (c % STAMP) - HALF).astype(F32)
    images = [None] * 12
    for k, sigma in enumerate(SIGMAS):
        lhs = split(
            jnp.concatenate(
                [rows[64 * k : 64 * k + 64, 256 * q : 256 * q + 256] for q in range(quads)], axis=0
            )
        )
        g = gauss_of(offset, sigma, same)
        for j in range(2):
            out = mm3(lhs, split(g * (offset * (1.0 / HALF)) if j else g))
            for i in range(2):
                images[4 * k + i + 2 * j] = jnp.concatenate(
                    [out[64 * q + 32 * i : 64 * q + 32 * i + 32] for q in range(quads)], axis=0
                )
    acc[...] = jnp.zeros_like(acc)
    good = gst[...]
    sci = sst[...]
    for k in range(12):
        weighted = images[k] * good
        acc[16 * k + 12 : 16 * k + 13, :] = jnp.sum(weighted * sci, axis=0, keepdims=True)
        for l in range(k + 1):
            value = jnp.sum(weighted * images[l], axis=0, keepdims=True)
            acc[16 * k + l : 16 * k + l + 1, :] = value
            if l < k:
                acc[16 * l + k : 16 * l + k + 1, :] = value
    n = acc.shape[0]
    summed = jnp.dot(acc[...], jnp.ones((128, 128), F32), precision=HIGHEST)
    r = lax.broadcasted_iota(jnp.int32, (n, 128), 0)
    c = lax.broadcasted_iota(jnp.int32, (n, 128), 1)
    summed = jnp.where(r % 16 == c, summed, 0.0)
    r = lax.broadcasted_iota(jnp.int32, (16, n), 0)
    c = lax.broadcasted_iota(jnp.int32, (16, n), 1)
    pick = jnp.where(c // 16 == r, 1.0, 0.0).astype(F32)
    out_ref[...] = jnp.dot(pick, summed, precision=HIGHEST)


def solve_system(system):
    r = lax.broadcasted_iota(jnp.int32, (16, 128), 0)
    c = lax.broadcasted_iota(jnp.int32, (16, 128), 1)
    diag = (r == c) & (r < 12)
    trace = jnp.sum(jnp.where(diag, system, 0.0), keepdims=True)
    m = system + jnp.where(diag, 0.05 * trace / 12.0, 0.0)
    for p in range(12):
        row = m[p : p + 1, :] / m[p : p + 1, p : p + 1]
        m = jnp.where(r == p, row, m - m[:, p : p + 1] * row)
    return m


def stacked_band(g):
    hi, lo = split(g)
    return jnp.concatenate([hi, lo, hi], axis=1)


def stacked_rows(x):
    hi, lo = split(x)
    return jnp.concatenate([hi, hi, lo], axis=0)


def block_starts(count):
    starts = list(range(0, count - BLOCK + 1, BLOCK))
    return starts if count % BLOCK == 0 else starts + [count - BLOCK]


def row_bands(bands):
    offset = band_offset(BLOCK, BLOCK + 2 * DH, 1, DH)
    for k, sigma in enumerate(SIGMAS):
        g = gauss_of(offset, sigma)
        for i in range(2):
            at = slice(BLOCK * (2 * k + i), BLOCK * (2 * k + i + 1))
            bands[at, :] = stacked_band(g * (offset * (1.0 / HALF)) if i else g)


def row_stage(start, tpad, phi, plo, bands):
    out = mm(bands[...], stacked_rows(tpad[start : start + BLOCK + 2 * DH, :]))
    for s in range(6):
        hi, lo = split(out[BLOCK * s : BLOCK * (s + 1)])
        phi[s, start : start + BLOCK, :] = hi
        plo[s, start : start + BLOCK, :] = lo


def apply_fit(tiles, system, halo_ref, sci_ref, det_ref, coef_ref, phi, plo, dpad):
    rows, cols = sci_ref.shape
    drows = rows + 2 * DH
    solved = solve_system(system)
    r = lax.broadcasted_iota(jnp.int32, (16, 128), 0)
    c = lax.broadcasted_iota(jnp.int32, (16, 128), 1)
    coef = jnp.sum(jnp.where(r == c, solved[:, 12:13], 0.0), axis=0, keepdims=True)
    coef_ref[...] = coef[:, :12]
    offset = band_offset(256 + 2 * PAD, 256, 0, PAD)
    scaled = offset * (1.0 / HALF)
    mats = []
    for k, sigma in enumerate(SIGMAS):
        g = gauss_of(offset, sigma)
        for i in range(2):
            a = solved[4 * k + i : 4 * k + i + 1, 12:13]
            b = solved[4 * k + i + 2 : 4 * k + i + 3, 12:13]
            mats.append(split(g * (a + b * scaled)))
    dpad[:, :PAD] = jnp.zeros((drows, PAD), F32)
    dpad[:, PAD + cols :] = jnp.zeros((drows, PAD), F32)
    above, below = inner_edges(tiles)
    for j in range(cols // 256):
        at = slice(256 * j, 256 * j + 256 + 2 * PAD)
        model = jnp.zeros((drows, 256), F32)
        for s in range(6):
            model = model + mm3((phi[s, :, at], plo[s, :, at]), mats[s])
        here = slice(256 * j, 256 * j + 256)
        to = slice(PAD + 256 * j, PAD + 256 * j + 256)
        dpad[:DH, to] = (halo_ref[:, here] - model[:DH]) * above
        dpad[DH : DH + rows, to] = sci_ref[:, here] - model[DH : DH + rows]
        dpad[DH + rows :, to] = (halo_ref[:, here] - model[DH + rows :]) * below
    psf_row = stacked_band(gauss_of(band_offset(BLOCK, BLOCK + 2 * DH, 1, DH), PSF))
    psf_col = split(gauss_of(offset, PSF))
    inner = [
        mm(psf_row, stacked_rows(dpad[start : start + BLOCK + 2 * DH, :]))
        for start in range(0, rows, BLOCK)
    ]
    for b in range(rows // 128):
        hi, lo = split(jnp.concatenate(inner[2 * b : 2 * b + 2], axis=0))
        for j in range(cols // 256):
            at = slice(256 * j, 256 * j + 256 + 2 * PAD)
            det_ref[128 * b : 128 * b + 128, 256 * j : 256 * j + 256] = mm3(
                (hi[:, at], lo[:, at]), psf_col
            )


def ring_place(count, paired):
    if not paired:
        return lambda e: e, lambda p: p
    half = count // 2

    def position(e):
        z, y = e // 2, e % 2
        return z + y * (count - 1 - 2 * z)

    def index(p):
        far = p // half
        return 2 * p * (1 - far) + far * (2 * (count - 1 - p) + 1)

    return position, index


def gather_kernel(count, paired, own_ref, sci_ref, blocks, edges, halo, ssem, rsem, esend, erecv, hsem, lsem):
    me = lax.axis_index("epoch")
    tile = lax.axis_index("tile")
    position, index = ring_place(count, paired)
    pos = position(me)
    ring = (index(lax.rem(pos + 1, count)), index(lax.rem(pos + count - 1, count)))
    other = 1 - tile
    barrier = pltpu.get_barrier_semaphore()
    for e in ring:
        pl.semaphore_signal(barrier, inc=1, device_id={"epoch": e}, device_id_type=MESH)
    pl.semaphore_signal(barrier, inc=1, device_id={"tile": other}, device_id_type=MESH)
    keep = pltpu.make_async_copy(own_ref, blocks.at[me], lsem)
    keep.start()
    pl.semaphore_wait(barrier, 3)
    rows = own_ref.shape[0]
    chunk = rows // CHUNKS

    def move(way, step, c, origin, src=None):
        at = pl.ds(c * chunk, chunk)
        return pltpu.make_async_remote_copy(
            src_ref=blocks.at[origin, at] if src is None else src.at[at],
            dst_ref=blocks.at[origin, at],
            send_sem=ssem.at[way, step, c],
            recv_sem=rsem.at[way, step, c],
            device_id={"epoch": ring[way]},
            device_id_type=MESH,
        )

    def edge(step, origin, src=None):
        at = pl.ds(pl.multiple_of(other * (rows - RH), 8), RH)
        return pltpu.make_async_remote_copy(
            src_ref=blocks.at[origin, at] if src is None else src.at[at],
            dst_ref=edges.at[origin],
            send_sem=esend.at[step],
            recv_sem=erecv.at[step],
            device_id={"tile": other},
            device_id_type=MESH,
        )

    reach = count // 2

    def has(way, step, c):
        return step < reach or count % 2 == 1 or (c < CHUNKS // 2) == (way == 0)

    started = []
    for c in range(CHUNKS):
        for way in range(2):
            if has(way, 1, c):
                started.append(move(way, 0, c, me, own_ref))
                started[-1].start()
    first = edge(0, me, own_ref)
    first.start()
    at = pl.ds(pl.multiple_of(other * (sci_ref.shape[0] - DH), 8), DH)
    science = pltpu.make_async_remote_copy(
        src_ref=sci_ref.at[at],
        dst_ref=halo,
        send_sem=hsem.at[0],
        recv_sem=hsem.at[1],
        device_id={"tile": other},
        device_id_type=MESH,
    )
    science.start()
    side = [first]
    for step in range(1, reach + 1):
        origins = [index(lax.rem(pos + (count - step if way == 0 else step), count)) for way in range(2)]
        halves = step == reach and count % 2 == 0
        for c in range(CHUNKS):
            for way in range(2):
                d = c if way == 0 or not halves else (c + CHUNKS // 2) % CHUNKS
                if not has(way, step, d):
                    continue
                move(way, step - 1, d, origins[way]).wait_recv()
                if step < reach and has(way, step + 1, d):
                    started.append(move(way, step, d, origins[way]))
                    started[-1].start()
        for origin in origins[:1] if halves else origins:
            side.append(edge(len(side), origin))
            side[-1].start()
    for copy in started:
        copy.wait_send()
    for copy in side:
        copy.wait()
    science.wait()
    keep.wait()


def fit_kernel(
    epochs, tiles, part, blocks_ref, edges_ref, halo_ref, sci_hbm, det_ref, coef_ref,
    tpad, sci_in, slots, phi, plo, dpad, bands, ssem, rsem, lsem, isem,
):
    count = epochs * tiles
    me = lax.axis_index("epoch") * tiles + lax.axis_index("tile")
    barrier = pltpu.get_barrier_semaphore()

    def where(d):
        peer = lax.rem(me + d, count)
        return {"epoch": peer // tiles, "tile": peer % tiles}

    def greet(d, _):
        pl.semaphore_signal(barrier, inc=1, device_id=where(d), device_id_type=MESH)
        return _

    lax.fori_loop(1, count, greet, 0)
    fill_padded(tiles, blocks_ref, edges_ref, tpad)
    fetch = pltpu.make_async_copy(sci_hbm, sci_in, isem)
    fetch.start()
    row_bands(bands)
    starts = block_starts(dpad.shape[0])
    for start in starts[:2]:
        row_stage(start, tpad, phi, plo, bands)
    keep = pltpu.make_async_copy(part, slots.at[me], lsem)
    keep.start()
    pl.semaphore_wait(barrier, count - 1)

    def copy(d, slot):
        return pltpu.make_async_remote_copy(
            src_ref=part,
            dst_ref=slots.at[slot],
            send_sem=ssem.at[d],
            recv_sem=rsem.at[d],
            device_id=where(d),
            device_id_type=MESH,
        )

    def send(d, _):
        copy(d, me).start()
        return _

    lax.fori_loop(1, count, send, 0)
    for start in starts[2:]:
        row_stage(start, tpad, phi, plo, bands)
    keep.wait()
    fetch.wait()

    def finish(d, _):
        made = copy(d, lax.rem(me + count - d, count))
        made.wait_send()
        made.wait_recv()
        return _

    lax.fori_loop(1, count, finish, 0)
    system = jnp.sum(slots[...], axis=0)
    apply_fit(tiles, system, halo_ref, sci_in, det_ref, coef_ref, phi, plo, dpad)


def vmem_specs(count):
    return [pl.BlockSpec(memory_space=pltpu.VMEM)] * count


def local(epochs, tiles, paired, template, science, flags, stamp_rows, stamp_cols):
    sci = science[0]
    rows, cols = sci.shape
    width = template.shape[1]
    ext_rows = rows + 2 * RH
    padded = cols + 2 * PAD
    stamps = stamp_rows.shape[1]
    reach = epochs // 2
    blocks, edges, halo = pl.pallas_call(
        functools.partial(gather_kernel, epochs, paired),
        out_shape=(
            jax.ShapeDtypeStruct((epochs, rows, width), F32),
            jax.ShapeDtypeStruct((epochs, RH, width), F32),
            jax.ShapeDtypeStruct((DH, cols), F32),
        ),
        in_specs=[pl.BlockSpec(memory_space=pl.ANY)] * 2,
        out_specs=tuple(vmem_specs(3)),
        scratch_shapes=[
            pltpu.SemaphoreType.DMA((2, reach, CHUNKS)),
            pltpu.SemaphoreType.DMA((2, reach, CHUNKS)),
            pltpu.SemaphoreType.DMA((epochs,)),
            pltpu.SemaphoreType.DMA((epochs,)),
            pltpu.SemaphoreType.DMA((2,)),
            pltpu.SemaphoreType.DMA,
        ],
        compiler_params=pltpu.CompilerParams(collective_id=0, has_side_effects=True),
        name="gather",
    )(template, sci)
    partial = pl.pallas_call(
        functools.partial(stamp_kernel, tiles),
        out_shape=jax.ShapeDtypeStruct((16, 128), F32),
        in_specs=[pl.BlockSpec(memory_space=pltpu.SMEM)] * 2 + vmem_specs(4),
        out_specs=pl.BlockSpec(memory_space=pltpu.VMEM),
        scratch_shapes=[
            pltpu.VMEM((ext_rows, padded), F32),
            pltpu.VMEM((48, 64 * stamps), F32),
            pltpu.VMEM((STAMP * stamps // 4, 128), F32),
            pltpu.VMEM((STAMP * stamps // 4, 128), F32),
            pltpu.VMEM((192, 128), F32),
        ],
        name="stamps",
    )(stamp_rows, stamp_cols, blocks, edges, sci, flags[0])
    drows = rows + 2 * DH
    detection, coefficients = pl.pallas_call(
        functools.partial(fit_kernel, epochs, tiles),
        out_shape=(
            jax.ShapeDtypeStruct((rows, cols), F32),
            jax.ShapeDtypeStruct((1, 12), F32),
        ),
        in_specs=[pl.BlockSpec(memory_space=pltpu.HBM)] + vmem_specs(3) + [pl.BlockSpec(memory_space=pl.ANY)],
        out_specs=tuple(vmem_specs(2)),
        scratch_shapes=[
            pltpu.VMEM((ext_rows, padded), F32),
            pltpu.VMEM((rows, cols), F32),
            pltpu.VMEM((epochs * tiles, 16, 128), F32),
            pltpu.VMEM((6, drows, padded), BF16),
            pltpu.VMEM((6, drows, padded), BF16),
            pltpu.VMEM((drows, padded), F32),
            pltpu.VMEM((6 * BLOCK, 3 * (BLOCK + 2 * DH)), BF16),
            pltpu.SemaphoreType.DMA((epochs * tiles,)),
            pltpu.SemaphoreType.DMA((epochs * tiles,)),
            pltpu.SemaphoreType.DMA,
            pltpu.SemaphoreType.DMA,
        ],
        compiler_params=pltpu.CompilerParams(
            collective_id=1, has_side_effects=True, vmem_limit_bytes=48 * 1024 * 1024
        ),
        name="fit",
    )(partial, blocks, edges, halo, sci)
    return (detection[None], coefficients.reshape(12))


def solution(mesh):
    line = mesh.devices[0, :, 0]
    columns = {tuple(getattr(d, "coords", (0, 0)))[:2] for d in line}
    paired = len(columns) == 2 and len(line) % 2 == 0
    return jax.shard_map(
        functools.partial(local, mesh.shape["epoch"], mesh.shape["tile"], paired),
        mesh=mesh,
        in_specs=(
            P(("patch", "tile"), "epoch"),
            P(("patch", "epoch"), "tile", None),
            P(("patch", "epoch"), "tile", None),
            P(("patch", "epoch"), "tile"),
            P(("patch", "epoch"), "tile"),
        ),
        out_specs=(P(("patch", "epoch"), "tile", None), P("patch")),
        check_vma=False,
    )
```
